768 devices in a mesh: pts: 96 (over x, y, z_hi), cells: 8 (over z_lo, core).
Axes of the slice: x: 4, y: 8, z: 12 (z_hi: 3, z_lo: 4; z = z_hi * 4 + z_lo), core: 2. Of those that a mesh axis runs over, the one named last changes fastest.
Arguments:
- codes: int32 [49152, 512], P(('pts', 'cells')), may hold values from -127 to 127
- exponents: int32 [49152], P(('pts', 'cells')), may hold values from 6 to 9
- centroids: bfloat16 [24576, 512], P('cells'), as said below
- counters: int32 [24576], P('cells'), may hold values from 0 to 4095
Outputs:
- cell_sums: float32 [8, 3072, 512], P('cells', 'pts')
- cell_mass: float32 [8, 3072], P('cells', 'pts')
The draws below stay inside these ranges and needn't reach their ends.
Inputs may be any that keep to these rules, and one draw needn't show every extreme that they name: `centroids`: centroids are real-valued with row scales that differ from row to row.
All inputs are finite; a program needn't handle non-finite values.
Results may differ from the reference program's by a relative error of at most 0.013.
Values may be sent and summed in bfloat16 or wider, within the bound.
A program may use at most 32 MiB of HBM per device.

```python
import jax
import jax.numpy as jnp
from jax import lax

D = 512
K = 24576
PTS = 49152
C_DEV = 3072
N_CELLS = 8


def draw_centroids(key, part):
    first = jax.random.fold_in(key, 11)
    second = jax.random.fold_in(key, 12)
    row_scale = jnp.exp(jax.random.uniform(second, (K, 1), jnp.float32, -1.2, 1.2))
    base = jax.random.normal(first, (K, D), jnp.float32)
    return (base * row_scale).astype(jnp.bfloat16)


def set_ends(drawn, key, smallest, high):
    shape = drawn.shape
    index_at = [jax.random.randint(jax.random.fold_in(key, axis), (), 0, shape[axis]) for axis in range(len(shape))]
    drawn = drawn.at[tuple(index_at)].set(smallest)
    longest = shape.index(max(shape))
    index_at[longest] = (index_at[longest] + 1) % shape[longest]
    return drawn.at[tuple(index_at)].set(high)


def setup_inputs(seed: int = 0) -> dict:
    key_list = jax.random.split(jax.random.key(seed), 5)
    return {
        "codes": set_ends(jax.random.randint(key_list[0], (PTS, D), -127, 128), jax.random.fold_in(key_list[0], 1), -127, 127).astype(jnp.int32),
        "exponents": set_ends(jax.random.randint(key_list[1], (PTS,), 6, 10), jax.random.fold_in(key_list[1], 1), 6, 9).astype(jnp.int32),
        "centroids": draw_centroids(jax.random.fold_in(key_list[4], 71), 0),
        "counters": set_ends(jax.random.randint(key_list[3], (K,), 0, 4096), jax.random.fold_in(key_list[3], 1), 0, 4095).astype(jnp.int32),
    }


def reference(codes, exponents, centroids, counters):
    points = (codes.astype(jnp.float32) * jnp.exp2(-exponents.astype(jnp.float32))[:, None]).astype(jnp.bfloat16)
    inverse = lax.rsqrt(counters.astype(jnp.float32) + 1.0)
    beta = 4.0 / D ** 0.5
    block = 512 if PTS % 512 == 0 else PTS
    blocks = points.reshape(PTS // block, block, D)

    def step(carry, rows):
        sums, mass = carry
        logits = jnp.dot(rows, centroids.T, preferred_element_type=jnp.float32) * beta
        top = lax.optimization_barrier(jnp.max(logits, axis=1, keepdims=True))
        expo = jnp.exp(logits - top)
        total = lax.optimization_barrier(jnp.sum(expo, axis=1))
        novel = jnp.dot(expo, inverse, preferred_element_type=jnp.float32)
        weight = novel / total
        share = (expo * (weight / total)[:, None]).astype(jnp.bfloat16)
        mass = mass + lax.optimization_barrier(jnp.sum(share.astype(jnp.float32), axis=0))
        sums = sums + jnp.dot(share.T, rows, preferred_element_type=jnp.float32)
        return ((sums, mass), None)
    init = (jnp.zeros((K, D), jnp.float32), jnp.zeros((K,), jnp.float32))
    (sums, mass), unused = lax.scan(step, init, blocks)
    return (sums.reshape(N_CELLS, C_DEV, D), mass.reshape(N_CELLS, C_DEV))
```

```python
import functools
import math

import jax
import jax.numpy as jnp
from jax import lax
from jax.experimental import pallas as pl
from jax.experimental.pallas import tpu as pltpu
from jax.sharding import PartitionSpec as P

X, Y, ZH, ZL, CORES = 4, 8, 3, 4, 2
MESH = pl.DeviceIdType.MESH
F32, BF16 = jnp.float32, jnp.bfloat16


def power_of_minus(e):
    value = jnp.ones(e.shape, F32)
    for bit in range(7):
        step = jnp.full(e.shape, 2.0 ** -(2**bit), F32)
        value = value * jnp.where(((e >> bit) & 1) == 1, step, 1.0)
    return value


def dot_nt(a, b):
    return lax.dot_general(a, b, (((1,), (1,)), ((), ())), preferred_element_type=F32)


def kernel(
    scale,
    codes_hbm, exps_ref, cent_hbm, counters_ref,
    sums_ref, mass_ref,
    codes, cent, pts, inv, tmp, logit, share, acc, massacc,
    stats, rm, y_out, y_in, m_out, my_in, z_out, z_in, mz_out, mz_in,
    load_sem, g_send, g_recv, s_send, s_recv, r_send, r_recv,
    y_send, y_recv, my_send, my_recv, z_send, z_recv, mz_send, mz_recv,
):
    p = lax.axis_index("pts")
    me = lax.axis_index("cells")
    x = lax.div(p, Y * ZH)
    y = lax.rem(lax.div(p, ZH), Y)
    zh = lax.rem(p, ZH)
    zl = lax.div(me, CORES)
    core = lax.rem(me, CORES)
    other = 1 - core
    peers = ZL * CORES
    rows, width = pts.shape[3:]
    chunk = CORES * rows
    slice_rows = cent.shape[1]
    y_rows, z_rows = y_in.shape[1], z_in.shape[1]

    def at_x(j):
        xx = lax.rem(x + j, X)
        return ((xx * Y + y) * ZH + zh, me)

    def at_y(k):
        yy = lax.rem(y + k, Y)
        return ((x * Y + yy) * ZH + zh, me)

    def at_z(k):
        return ((x * Y + y) * ZH + lax.rem(zh + k, ZH), me)

    sibling = (p, zl * CORES + other)

    load_codes = pltpu.make_async_copy(codes_hbm, codes, load_sem.at[0])
    load_cent = pltpu.make_async_copy(cent_hbm, cent, load_sem.at[1])
    load_codes.start()
    load_cent.start()

    barrier = pltpu.get_barrier_semaphore()

    def greet(device):
        pl.semaphore_signal(barrier, inc=1, device_id=device, device_id_type=MESH)

    for k in range(1, Y):
        greet(at_y(k))
    for k in range(1, ZH):
        greet(at_z(k))
    for k in range(1, peers):
        greet((p, lax.rem(me + k, peers)))
    for j in range(1, X):
        greet(at_x(j))

    n_exp = exps_ref.shape[1]
    powers = power_of_minus(exps_ref[...])
    diagonal = lax.broadcasted_iota(jnp.int32, (n_exp, n_exp), 0) == lax.broadcasted_iota(
        jnp.int32, (n_exp, n_exp), 1
    )
    column = jnp.sum(jnp.where(diagonal, powers, 0.0), axis=1, keepdims=True)
    load_codes.wait()
    pts[x, zl, core] = (codes[...].astype(F32) * column).astype(BF16)

    pl.semaphore_wait(barrier, (Y - 1) + (ZH - 1) + (peers - 1) + (X - 1))

    def block(xx, zz, cc, device, sem):
        return pltpu.make_async_remote_copy(
            src_ref=pts.at[xx, zz, cc], dst_ref=pts.at[xx, zz, cc],
            send_sem=g_send.at[sem], recv_sem=g_recv.at[xx, zz, cc],
            device_id=device, device_id_type=MESH,
        )

    block(x, zl, core, sibling, 0).start()
    for k in range(1, ZL):
        block(x, zl, core, (p, lax.rem(zl + k, ZL) * CORES + core), k).start()
    for j in range(1, X):
        block(x, zl, core, at_x(j), ZL - 1 + j).start()
    sem_zl = ZL + X - 1

    square = (128, 128)
    eye = lax.broadcasted_iota(jnp.int32, square, 0) == lax.broadcasted_iota(jnp.int32, square, 1)

    def spread(g, carry):
        row = lax.rsqrt(counters_ref[pl.ds(g, 1), :].astype(F32) + 1.0)
        col = jnp.sum(jnp.where(eye, row, 0.0), axis=1, keepdims=True)
        inv[pl.ds(pl.multiple_of(g * 128, 128), 128), :] = jnp.broadcast_to(col, square)
        return carry

    lax.fori_loop(0, counters_ref.shape[0], spread, 0)
    load_cent.wait()

    def stat_copy(src, zz, k):
        return pltpu.make_async_remote_copy(
            src_ref=stats.at[src, zz], dst_ref=stats.at[src, zz],
            send_sem=s_send.at[k, zz], recv_sem=s_recv.at[src, zz],
            device_id=(p, lax.rem(me + k, peers)), device_id_type=MESH,
        )

    def local_stats(zz):
        points = pts[x, zz].reshape(chunk, width)

        def product(s, top):
            part = dot_nt(cent[s], points)
            tmp[s] = part
            return jnp.maximum(top, jnp.max(part, axis=0, keepdims=True))

        top = lax.fori_loop(0, X, product, jnp.full((1, chunk), -jnp.inf, F32))
        shift = top * scale

        def add_up(s, sums):
            expo = jnp.exp2(tmp[s] * scale - shift)
            weights = inv[pl.ds(pl.multiple_of(s * slice_rows, 128), slice_rows), :]
            return (
                sums[0] + jnp.sum(expo, axis=0, keepdims=True),
                sums[1] + jnp.sum(expo * weights, axis=0, keepdims=True),
            )

        zero = jnp.zeros((1, chunk), F32)
        total, novel = lax.fori_loop(0, X, add_up, (zero, zero))
        logit[x, :, pl.ds(pl.multiple_of(zz * chunk, 128), chunk)] = tmp[x]
        stats[me, zz, 0:1, :] = top
        stats[me, zz, 1:2, :] = total
        stats[me, zz, 2:3, :] = novel

        def send(k, carry):
            stat_copy(me, zz, k).start()
            return carry

        lax.fori_loop(1, peers, send, 0)

    block(x, zl, other, sibling, 0).wait_recv()
    local_stats(zl)
    if ZL == 4:
        first = zl + 1 - 2 * lax.div(zl, 2)
        last = 3 - 3 * lax.div(zl, 2)
        order = [first, 6 - zl - first - last, last]
    else:
        order = [lax.rem(zl + k, ZL) for k in range(1, ZL)]
    for k, zz in enumerate(order):
        block(x, zz, core, sibling, 0).wait_recv()
        for j in range(1, X):
            block(x, zz, core, at_x(j), sem_zl + k * X + j).start()
        block(x, zz, core, sibling, sem_zl + k * X).start()
        block(x, zz, other, sibling, 0).wait_recv()
        local_stats(zz)
    sem_x = sem_zl + (ZL - 1) * X

    x_order = [1, 3, 2] if X == 4 else list(range(1, X))
    for i, j in enumerate(x_order):
        xx = lax.rem(x + j, X)

        def pass_on(zz, carry, i=i, xx=xx):
            block(xx, zz, core, sibling, 0).wait_recv()
            block(xx, zz, core, sibling, sem_x + i * ZL + zz).start()
            return carry

        lax.fori_loop(0, ZL, pass_on, 0)
    for j in x_order:
        xx = lax.rem(x + j, X)

        def arrived(zz, carry, xx=xx):
            block(xx, zz, other, sibling, 0).wait_recv()
            return carry

        lax.fori_loop(0, ZL, arrived, 0)
        logit[xx] = dot_nt(cent[x], pts[xx].reshape(ZL * chunk, width))

    def stats_in(k, carry):
        src = lax.rem(me + k, peers)

        def one(zz, inner):
            stat_copy(src, zz, k).wait_recv()
            return inner

        return lax.fori_loop(0, ZL, one, carry)

    lax.fori_loop(1, peers, stats_in, 0)

    def combine(zz, carry):
        tops = stats[:, zz, 0, :]
        top = jnp.max(tops, axis=0, keepdims=True)
        ratio = jnp.exp2((tops - top) * scale)
        total = jnp.sum(stats[:, zz, 1, :] * ratio, axis=0, keepdims=True)
        novel = jnp.sum(stats[:, zz, 2, :] * ratio, axis=0, keepdims=True)
        rm[x, zz, 0:1, :] = top * scale
        rm[x, zz, 1:2, :] = novel / total / total
        return carry

    lax.fori_loop(0, ZL, combine, 0)

    def rm_copy(src, j):
        return pltpu.make_async_remote_copy(
            src_ref=rm.at[src], dst_ref=rm.at[src],
            send_sem=r_send.at[j], recv_sem=r_recv.at[src],
            device_id=at_x(j), device_id_type=MESH,
        )

    for j in range(1, X):
        rm_copy(x, j).start()

    acc[...] = jnp.zeros(acc.shape, F32)
    massacc[...] = jnp.zeros(massacc.shape, F32)

    def accumulate(xx):
        for zz in range(ZL):
            lanes = slice(zz * chunk, (zz + 1) * chunk)
            shift, factor = rm[xx, zz, 0:1, :], rm[xx, zz, 1:2, :]
            part = (jnp.exp2(logit[xx, :, lanes] * scale - shift) * factor).astype(BF16)
            share[:, lanes] = part
            massacc[...] += part.astype(F32)
        acc[...] += jnp.dot(
            share[...], pts[xx].reshape(ZL * chunk, width), preferred_element_type=F32
        )

    accumulate(x)
    for j in x_order:
        xx = lax.rem(x + j, X)
        rm_copy(xx, j).wait_recv()
        accumulate(xx)

    def y_copy(src, k, dst):
        return pltpu.make_async_remote_copy(
            src_ref=y_out.at[dst], dst_ref=y_in.at[src],
            send_sem=y_send.at[k], recv_sem=y_recv.at[src],
            device_id=at_y(k), device_id_type=MESH,
        )

    def my_copy(src, k):
        return pltpu.make_async_remote_copy(
            src_ref=m_out, dst_ref=my_in.at[src],
            send_sem=my_send.at[k], recv_sem=my_recv.at[src],
            device_id=at_y(k), device_id_type=MESH,
        )

    def y_start(k, carry):
        dst = lax.rem(y + k, Y)
        y_out[dst] = acc[pl.ds(pl.multiple_of(dst * y_rows, 16), y_rows), :].astype(BF16)
        y_copy(y, k, dst).start()
        return carry

    lax.fori_loop(1, Y, y_start, 0)

    m_out[...] = jnp.zeros(m_out.shape, F32)
    for g in range(slice_rows // 128):
        col = jnp.sum(massacc[g * 128 : (g + 1) * 128, :], axis=1, keepdims=True)
        m_out[g : g + 1, :] = jnp.sum(jnp.where(eye, col, 0.0), axis=0, keepdims=True)

    def my_start(k, carry):
        my_copy(y, k).start()
        return carry

    lax.fori_loop(1, Y, my_start, 0)

    own = pl.ds(pl.multiple_of(y * y_rows, 16), y_rows)

    def y_add(k, total):
        src = lax.rem(y + k, Y)
        y_copy(src, k, src).wait_recv()
        acc[own, :] += y_in[src].astype(F32)
        my_copy(src, k).wait_recv()
        return total + my_in[src]

    mass = lax.fori_loop(1, Y, y_add, m_out[...])

    def z_copy(src, k, dst):
        return pltpu.make_async_remote_copy(
            src_ref=z_out.at[dst], dst_ref=z_in.at[src],
            send_sem=z_send.at[k], recv_sem=z_recv.at[src],
            device_id=at_z(k), device_id_type=MESH,
        )

    def mz_copy(src, k):
        return pltpu.make_async_remote_copy(
            src_ref=mz_out, dst_ref=mz_in.at[src],
            send_sem=mz_send.at[k], recv_sem=mz_recv.at[src],
            device_id=at_z(k), device_id_type=MESH,
        )

    mz_out[...] = mass
    for k in range(1, ZH):
        dst = lax.rem(zh + k, ZH)
        begin = y * y_rows + dst * z_rows
        z_out[dst] = acc[pl.ds(pl.multiple_of(begin, 16), z_rows), :].astype(BF16)
        z_copy(zh, k, dst).start()
        mz_copy(zh, k).start()
    begin = y * y_rows + zh * z_rows
    result = acc[pl.ds(pl.multiple_of(begin, 16), z_rows), :]
    for k in range(1, ZH):
        src = lax.rem(zh + k, ZH)
        z_copy(src, k, src).wait_recv()
        mz_copy(src, k).wait_recv()
        result = result + z_in[src].astype(F32)
        mass = mass + mz_in[src]
    sums_ref[...] = result

    per_row = 128 // z_rows
    place = y * ZH + zh
    line = lax.div(place, per_row)
    which = lax.rem(place, per_row)
    at_line = lax.broadcasted_iota(jnp.int32, mass.shape, 0) == line
    picked = jnp.sum(jnp.where(at_line, mass, 0.0), axis=0, keepdims=True)
    answer = jnp.zeros((1, z_rows), F32)
    for q in range(per_row):
        answer = jnp.where(which == q, picked[:, q * z_rows : (q + 1) * z_rows], answer)
    mass_ref[...] = answer

    def sent_block(i, carry):
        block(x, zl, core, sibling, i).wait_send()
        return carry

    lax.fori_loop(0, g_send.shape[0], sent_block, 0)

    def sent_stats(k, carry):
        def one(zz, inner):
            stat_copy(me, zz, k).wait_send()
            return inner

        return lax.fori_loop(0, ZL, one, carry)

    lax.fori_loop(1, peers, sent_stats, 0)
    for j in range(1, X):
        rm_copy(x, j).wait_send()

    def sent_y(k, carry):
        y_copy(y, k, lax.rem(y + k, Y)).wait_send()
        my_copy(y, k).wait_send()
        return carry

    lax.fori_loop(1, Y, sent_y, 0)
    for k in range(1, ZH):
        z_copy(zh, k, lax.rem(zh + k, ZH)).wait_send()
        mz_copy(zh, k).wait_send()


def body(codes, exponents, centroids, counters):
    rows, width = codes.shape
    cells = centroids.shape[0]
    slice_rows = cells // X
    y_rows = slice_rows // Y
    z_rows = y_rows // ZH
    chunk = CORES * rows
    line = ZL * chunk
    peers = ZL * CORES
    scale = 4.0 / math.sqrt(width) * math.log2(math.e)
    vmem, dma = pltpu.VMEM, pltpu.SemaphoreType.DMA
    sums, mass = pl.pallas_call(
        functools.partial(kernel, scale),
        out_shape=(
            jax.ShapeDtypeStruct((z_rows, width), F32),
            jax.ShapeDtypeStruct((1, z_rows), F32),
        ),
        in_specs=[
            pl.BlockSpec(memory_space=pl.ANY),
            pl.BlockSpec(memory_space=vmem),
            pl.BlockSpec(memory_space=pl.ANY),
            pl.BlockSpec(memory_space=vmem),
        ],
        out_specs=(pl.BlockSpec(memory_space=vmem), pl.BlockSpec(memory_space=vmem)),
        scratch_shapes=[
            vmem((rows, width), jnp.int32),
            vmem((X, slice_rows, width), BF16),
            vmem((X, ZL, CORES, rows, width), BF16),
            vmem((cells, 128), F32),
            vmem((X, slice_rows, chunk), F32),
            vmem((X, slice_rows, line), F32),
            vmem((slice_rows, line), BF16),
            vmem((slice_rows, width), F32),
            vmem((slice_rows, chunk), F32),
            vmem((peers, ZL, 8, chunk), F32),
            vmem((X, ZL, 8, chunk), F32),
            vmem((Y, y_rows, width), BF16),
            vmem((Y, y_rows, width), BF16),
            vmem((8, 128), F32),
            vmem((Y, 8, 128), F32),
            vmem((ZH, z_rows, width), BF16),
            vmem((ZH, z_rows, width), BF16),
            vmem((8, 128), F32),
            vmem((ZH, 8, 128), F32),
            dma((2,)),
            dma((X + ZL - 1 + (ZL - 1) * X + (X - 1) * ZL,)),
            dma((X, ZL, CORES)),
            dma((peers, ZL)),
            dma((peers, ZL)),
            dma((X,)),
            dma((X,)),
            dma((Y,)),
            dma((Y,)),
            dma((Y,)),
            dma((Y,)),
            dma((ZH,)),
            dma((ZH,)),
            dma((ZH,)),
            dma((ZH,)),
        ],
        compiler_params=pltpu.CompilerParams(
            collective_id=0, has_side_effects=True, vmem_limit_bytes=48 << 20
        ),
    )(
        codes,
        exponents.reshape(1, rows),
        centroids.reshape(X, slice_rows, width),
        counters.reshape(cells // 128, 128),
    )
    return sums[None], mass


def solution(mesh):
    in_specs = (P(("pts", "cells"), None), P(("pts", "cells")), P("cells", None), P("cells"))
    out_specs = (P("cells", "pts", None), P("cells", "pts"))
    return jax.shard_map(body, mesh=mesh, in_specs=in_specs, out_specs=out_specs, check_vma=False)
```

```python
import functools
import math

import jax
import jax.numpy as jnp
from jax import lax
from jax.experimental import pallas as pl
from jax.experimental.pallas import tpu as pltpu
from jax.sharding import PartitionSpec as P

X, Y, ZH, ZL, CORES = 4, 8, 3, 4, 2
NY, NZ = 2, 2
MESH = pl.DeviceIdType.MESH
F32, BF16 = jnp.float32, jnp.bfloat16


def power_of_minus(e):
    value = jnp.ones(e.shape, F32)
    for bit in range(7):
        step = jnp.full(e.shape, 2.0 ** -(2**bit), F32)
        value = value * jnp.where(((e >> bit) & 1) == 1, step, 1.0)
    return value


def dot_nt(a, b):
    return lax.dot_general(a, b, (((1,), (1,)), ((), ())), preferred_element_type=F32)


def kernel(
    scale,
    codes_hbm, exps_hbm, cent_hbm, counters_hbm,
    sums_ref, mass_ref,
    codes, exps, cent, counters, pts, inv, tmp, logit, share, acc, massacc,
    stats, rm, y_out, y_in, y_sum, yz_out, yz_in, z_out, z_in, z_sum, zy_out, zy_in,
    m_out, my_in, mz_out, mz_in,
    load_sem, g_send, g_recv, s_send, s_recv, r_send, r_recv,
    y_send, y_recv, yz_send, yz_recv, z_send, z_recv, zy_send, zy_recv,
    my_send, my_recv, mz_send, mz_recv,
):
    p = lax.axis_index("pts")
    me = lax.axis_index("cells")
    x = lax.div(p, Y * ZH)
    y = lax.rem(lax.div(p, ZH), Y)
    zh = lax.rem(p, ZH)
    zl = lax.div(me, CORES)
    core = lax.rem(me, CORES)
    other = 1 - core
    peers = ZL * CORES
    half_chips = ZL // 2
    half = lax.div(zl, half_chips)
    rows, width = pts.shape[3:]
    line = ZL * CORES * rows
    lanes = line // 2
    slice_rows = cent.shape[1]
    z_rows = acc.shape[2]
    piece = width // (NY + NZ)

    def at_x(j):
        return ((lax.rem(x + j, X) * Y + y) * ZH + zh, me)

    def at_y(k):
        return ((x * Y + lax.rem(y + k, Y)) * ZH + zh, me)

    def at_z(k):
        return ((x * Y + y) * ZH + lax.rem(zh + k, ZH), me)

    def at_cells(k):
        return (p, lax.rem(me + k, peers))

    sibling = (p, zl * CORES + other)

    def send(src, dst, send_sem, recv_sem, device):
        return pltpu.make_async_remote_copy(
            src_ref=src, dst_ref=dst, send_sem=send_sem, recv_sem=recv_sem,
            device_id=device, device_id_type=MESH,
        )

    loads = [
        pltpu.make_async_copy(src, dst, load_sem.at[i])
        for i, (src, dst) in enumerate(
            ((exps_hbm, exps), (codes_hbm, codes), (counters_hbm, counters), (cent_hbm, cent))
        )
    ]
    for load in loads:
        load.start()

    barrier = pltpu.get_barrier_semaphore()

    def greet(device):
        pl.semaphore_signal(barrier, inc=1, device_id=device, device_id_type=MESH)

    for k in range(1, peers):
        greet(at_cells(k))
    for j in range(1, X):
        greet(at_x(j))
    for k in range(1, ZH):
        greet(at_z(k))
    for k in range(1, Y):
        greet(at_y(k))

    n_exp = exps.shape[1]
    diagonal = lax.broadcasted_iota(jnp.int32, (n_exp, n_exp), 0) == lax.broadcasted_iota(
        jnp.int32, (n_exp, n_exp), 1
    )
    loads[0].wait()
    powers = power_of_minus(exps[...])
    column = jnp.sum(jnp.where(diagonal, powers, 0.0), axis=1, keepdims=True)
    loads[1].wait()
    pts[x, zl, core] = (codes[...].astype(F32) * column).astype(BF16)

    pl.semaphore_wait(barrier, (Y - 1) + (ZH - 1) + (peers - 1) + (X - 1))

    def block(xx, zz, cc, device, sem):
        ref = pts.at[xx, zz, cc]
        return send(ref, ref, g_send.at[sem], g_recv.at[xx, zz, cc], device)

    for k in range(1, ZL):
        block(x, zl, core, (p, lax.rem(zl + k, ZL) * CORES + core), k).start()
    block(x, zl, core, sibling, 0).start()
    for j in range(1, X):
        block(x, zl, core, at_x(j), ZL - 1 + j).start()
    sem_zl = ZL + X - 1
    sem_x = sem_zl + (ZL - 1) * X

    square = (128, 128)
    eye = lax.broadcasted_iota(jnp.int32, square, 0) == lax.broadcasted_iota(jnp.int32, square, 1)
    loads[2].wait()

    def spread(g, carry):
        row = lax.rsqrt(counters[pl.ds(g, 1), :].astype(F32) + 1.0)
        col = jnp.sum(jnp.where(eye, row, 0.0), axis=1, keepdims=True)
        inv[pl.ds(pl.multiple_of(g * 128, 128), 128), :] = jnp.broadcast_to(col, square)
        return carry

    lax.fori_loop(0, counters.shape[0], spread, 0)
    loads[3].wait()

    def stat_copy(src, hh, k):
        ref = stats.at[src, hh]
        return send(ref, ref, s_send.at[k, hh], s_recv.at[src, hh], at_cells(k))

    def points_of(xx, hh):
        return pts[xx, pl.ds(hh * half_chips, half_chips)].reshape(lanes, width)

    def local_stats(hh):
        points = points_of(x, hh)

        def product(s, top):
            part = dot_nt(cent[s], points)
            tmp[s] = part
            return jnp.maximum(top, jnp.max(part, axis=0, keepdims=True))

        top = lax.fori_loop(0, X, product, jnp.full((1, lanes), -jnp.inf, F32))
        shift = top * scale

        def add_up(s, sums):
            expo = jnp.exp2(tmp[s] * scale - shift)
            weights = inv[pl.ds(pl.multiple_of(s * slice_rows, 128), slice_rows), :]
            weights = jnp.concatenate([weights] * (lanes // 128), axis=1)
            return (
                sums[0] + jnp.sum(expo, axis=0, keepdims=True),
                sums[1] + jnp.sum(expo * weights, axis=0, keepdims=True),
            )

        zero = jnp.zeros((1, lanes), F32)
        total, novel = lax.fori_loop(0, X, add_up, (zero, zero))
        stats[me, hh, 0:1, :] = top
        stats[me, hh, 1:2, :] = total
        stats[me, hh, 2:3, :] = novel

        def start(k, carry):
            stat_copy(me, hh, k).start()
            return carry

        lax.fori_loop(1, peers, start, 0)
        logit[x, :, pl.ds(pl.multiple_of(hh * lanes, 128), lanes)] = tmp[x]

    def forward(zz, slot):
        block(x, zz, core, sibling, 0).wait_recv()
        for j in range(1, X):
            block(x, zz, core, at_x(j), sem_zl + slot * X + j).start()
        block(x, zz, core, sibling, sem_zl + slot * X).start()

    begin = half * half_chips
    for k in range(1, half_chips):
        forward(begin + lax.rem(zl - begin + k, half_chips), k - 1)
    for k in range(half_chips):
        block(x, begin + k, other, sibling, 0).wait_recv()
    local_stats(half)
    begin = (1 - half) * half_chips
    for k in range(half_chips):
        forward(begin + k, half_chips - 1 + k)
    for k in range(half_chips):
        block(x, begin + k, other, sibling, 0).wait_recv()
    local_stats(1 - half)

    x_order = [1, 3, 2] if X == 4 else list(range(1, X))
    for i, j in enumerate(x_order):
        xx = lax.rem(x + j, X)

        def pass_on(zz, carry, i=i, xx=xx):
            block(xx, zz, core, sibling, 0).wait_recv()
            block(xx, zz, core, sibling, sem_x + i * ZL + zz).start()
            return carry

        lax.fori_loop(0, ZL, pass_on, 0)
    for j in x_order:
        xx = lax.rem(x + j, X)

        def arrived(zz, carry, xx=xx):
            block(xx, zz, other, sibling, 0).wait_recv()
            return carry

        lax.fori_loop(0, ZL, arrived, 0)
        logit[xx] = dot_nt(cent[x], pts[xx].reshape(line, width))

    def stats_in(k, carry):
        src = lax.rem(me + k, peers)
        for hh in range(2):
            stat_copy(src, hh, k).wait_recv()
        return carry

    lax.fori_loop(1, peers, stats_in, 0)
    for hh in range(2):
        here = slice(hh * lanes, (hh + 1) * lanes)
        tops = stats[:, hh, 0, :]
        top = jnp.max(tops, axis=0, keepdims=True)
        ratio = jnp.exp2((tops - top) * scale)
        total = jnp.sum(stats[:, hh, 1, :] * ratio, axis=0, keepdims=True)
        novel = jnp.sum(stats[:, hh, 2, :] * ratio, axis=0, keepdims=True)
        rm[x, 0:1, here] = top * scale
        rm[x, 1:2, here] = novel / total / total

    def rm_copy(src, j):
        return send(rm.at[src], rm.at[src], r_send.at[j], r_recv.at[src], at_x(j))

    for j in range(1, X):
        rm_copy(x, j).start()

    acc[...] = jnp.zeros(acc.shape, F32)
    massacc[...] = jnp.zeros(massacc.shape, F32)

    def accumulate(xx):
        for q in range(line // 128):
            here = slice(q * 128, (q + 1) * 128)
            shift, factor = rm[xx, 0:1, here], rm[xx, 1:2, here]
            part = (jnp.exp2(logit[xx, :, here] * scale - shift) * factor).astype(BF16)
            share[:, here] = part
            massacc[...] += part.astype(F32)
        acc[...] += jnp.dot(
            share[...], pts[xx].reshape(line, width), preferred_element_type=F32
        ).reshape(acc.shape)

    accumulate(x)
    for j in x_order:
        xx = lax.rem(x + j, X)
        rm_copy(xx, j).wait_recv()
        accumulate(xx)

    def y_copy(q, src, k, dst):
        return send(y_out.at[q, dst], y_in.at[q, src], y_send.at[q, k], y_recv.at[q, src], at_y(k))

    def z_copy(q, src, k, dst):
        return send(z_out.at[q, dst], z_in.at[q, src], z_send.at[q, k], z_recv.at[q, src], at_z(k))

    def yz_copy(q, src, k, dst):
        return send(
            yz_out.at[q, dst], yz_in.at[q, src], yz_send.at[q, k], yz_recv.at[q, src], at_z(k)
        )

    def zy_copy(q, src, k, dst):
        return send(
            zy_out.at[q, dst], zy_in.at[q, src], zy_send.at[q, k], zy_recv.at[q, src], at_y(k)
        )

    def my_copy(src, k):
        return send(m_out, my_in.at[src], my_send.at[k], my_recv.at[src], at_y(k))

    def mz_copy(src, k):
        return send(mz_out, mz_in.at[src], mz_send.at[k], mz_recv.at[src], at_z(k))

    def columns(q):
        return slice(q * piece, (q + 1) * piece)

    def over_y(step, first=0):
        return lax.fori_loop(1, Y, step, first)

    def over_z(step, first=0):
        return lax.fori_loop(1, ZH, step, first)

    def y_first(q):
        def start(k, carry):
            dst = lax.rem(y + k, Y)
            y_out[q, dst] = acc[dst, :, :, columns(q)].astype(BF16)
            y_copy(q, y, k, dst).start()
            return carry

        over_y(start)

    def z_first(q):
        def start(k, carry):
            dst = lax.rem(zh + k, ZH)
            z_out[q, dst] = acc[:, dst, :, columns(NY + q)].astype(BF16)
            z_copy(q, zh, k, dst).start()
            return carry

        over_z(start)

    def y_then_z(q):
        def add(k, total):
            src = lax.rem(y + k, Y)
            y_copy(q, src, k, src).wait_recv()
            return total + y_in[q, src].astype(F32)

        y_sum[q] = over_y(add, acc[y, :, :, columns(q)])

        def start(k, carry):
            dst = lax.rem(zh + k, ZH)
            yz_out[q, dst] = y_sum[q, dst].astype(BF16)
            yz_copy(q, zh, k, dst).start()
            return carry

        over_z(start)

    def z_then_y(q):
        def add(k, carry):
            src = lax.rem(zh + k, ZH)
            z_copy(q, src, k, src).wait_recv()
            z_sum[q] += z_in[q, src].astype(F32)
            return carry

        z_sum[q] = acc[:, zh, :, columns(NY + q)]
        over_z(add)

        def start(k, carry):
            dst = lax.rem(y + k, Y)
            zy_out[q, dst] = z_sum[q, dst].astype(BF16)
            zy_copy(q, y, k, dst).start()
            return carry

        over_y(start)

    def finish_y(q):
        def add(k, total):
            src = lax.rem(zh + k, ZH)
            yz_copy(q, src, k, src).wait_recv()
            return total + yz_in[q, src].astype(F32)

        sums_ref[:, columns(q)] = over_z(add, y_sum[q, zh])

    def finish_z(q):
        def add(k, total):
            src = lax.rem(y + k, Y)
            zy_copy(q, src, k, src).wait_recv()
            return total + zy_in[q, src].astype(F32)

        sums_ref[:, columns(NY + q)] = over_y(add, z_sum[q, y])

    for q in range(max(NY, NZ)):
        if q < NY:
            y_first(q)
        if q < NZ:
            z_first(q)

    m_out[...] = jnp.zeros(m_out.shape, F32)
    for g in range(slice_rows // 128):
        col = jnp.sum(massacc[g * 128 : (g + 1) * 128, :], axis=1, keepdims=True)
        m_out[g : g + 1, :] = jnp.sum(jnp.where(eye, col, 0.0), axis=0, keepdims=True)

    def my_start(k, carry):
        my_copy(y, k).start()
        return carry

    over_y(my_start)

    for q in range(max(NY, NZ)):
        if q < NY:
            y_then_z(q)
        if q < NZ:
            z_then_y(q)
        if q == 0:

            def my_add(k, total):
                src = lax.rem(y + k, Y)
                my_copy(src, k).wait_recv()
                return total + my_in[src]

            mass = over_y(my_add, m_out[...])
            mz_out[...] = mass

            def mz_start(k, carry):
                mz_copy(zh, k).start()
                return carry

            over_z(mz_start)

    def mz_add(k, total):
        src = lax.rem(zh + k, ZH)
        mz_copy(src, k).wait_recv()
        return total + mz_in[src]

    mass = over_z(mz_add, mass)
    per_row = 128 // z_rows
    place = y * ZH + zh
    at_line = lax.broadcasted_iota(jnp.int32, mass.shape, 0) == lax.div(place, per_row)
    picked = jnp.sum(jnp.where(at_line, mass, 0.0), axis=0, keepdims=True)
    which = lax.rem(place, per_row)
    answer = jnp.zeros((1, z_rows), F32)
    for q in range(per_row):
        answer = jnp.where(which == q, picked[:, q * z_rows : (q + 1) * z_rows], answer)
    mass_ref[...] = answer

    for q in range(max(NY, NZ)):
        if q < NY:
            finish_y(q)
        if q < NZ:
            finish_z(q)

    def sent_block(i, carry):
        block(x, zl, core, sibling, i).wait_send()
        return carry

    lax.fori_loop(0, g_send.shape[0], sent_block, 0)

    def sent_stats(k, carry):
        for hh in range(2):
            stat_copy(me, hh, k).wait_send()
        return carry

    lax.fori_loop(1, peers, sent_stats, 0)
    for j in range(1, X):
        rm_copy(x, j).wait_send()

    def sent_y(k, carry):
        dst = lax.rem(y + k, Y)
        for q in range(NY):
            y_copy(q, y, k, dst).wait_send()
        for q in range(NZ):
            zy_copy(q, y, k, dst).wait_send()
        my_copy(y, k).wait_send()
        return carry

    over_y(sent_y)

    def sent_z(k, carry):
        dst = lax.rem(zh + k, ZH)
        for q in range(NY):
            yz_copy(q, zh, k, dst).wait_send()
        for q in range(NZ):
            z_copy(q, zh, k, dst).wait_send()
        mz_copy(zh, k).wait_send()
        return carry

    over_z(sent_z)


def body(codes, exponents, centroids, counters):
    rows, width = codes.shape
    cells = centroids.shape[0]
    slice_rows = cells // X
    z_rows = slice_rows // Y // ZH
    line = ZL * CORES * rows
    lanes = line // 2
    peers = ZL * CORES
    piece = width // (NY + NZ)
    scale = 4.0 / math.sqrt(width) * math.log2(math.e)
    vmem, dma = pltpu.VMEM, pltpu.SemaphoreType.DMA
    hbm = pl.BlockSpec(memory_space=pltpu.HBM)
    sums, mass = pl.pallas_call(
        functools.partial(kernel, scale),
        out_shape=(
            jax.ShapeDtypeStruct((z_rows, width), F32),
            jax.ShapeDtypeStruct((1, z_rows), F32),
        ),
        in_specs=[hbm] * 4,
        out_specs=(pl.BlockSpec(memory_space=vmem), pl.BlockSpec(memory_space=vmem)),
        scratch_shapes=[
            vmem((rows, width), jnp.int32),
            vmem((1, rows), jnp.int32),
            vmem((X, slice_rows, width), BF16),
            vmem((cells // 128, 128), jnp.int32),
            vmem((X, ZL, CORES, rows, width), BF16),
            vmem((cells, 128), F32),
            vmem((X, slice_rows, lanes), F32),
            vmem((X, slice_rows, line), F32),
            vmem((slice_rows, line), BF16),
            vmem((Y, ZH, z_rows, width), F32),
            vmem((slice_rows, 128), F32),
            vmem((peers, 2, 8, lanes), F32),
            vmem((X, 8, line), F32),
            vmem((NY, Y, ZH, z_rows, piece), BF16),
            vmem((NY, Y, ZH, z_rows, piece), BF16),
            vmem((NY, ZH, z_rows, piece), F32),
            vmem((NY, ZH, z_rows, piece), BF16),
            vmem((NY, ZH, z_rows, piece), BF16),
            vmem((NZ, ZH, Y, z_rows, piece), BF16),
            vmem((NZ, ZH, Y, z_rows, piece), BF16),
            vmem((NZ, Y, z_rows, piece), F32),
            vmem((NZ, Y, z_rows, piece), BF16),
            vmem((NZ, Y, z_rows, piece), BF16),
            vmem((8, 128), F32),
            vmem((Y, 8, 128), F32),
            vmem((8, 128), F32),
            vmem((ZH, 8, 128), F32),
            dma((4,)),
            dma((X + ZL - 1 + (ZL - 1) * X + (X - 1) * ZL,)),
            dma((X, ZL, CORES)),
            dma((peers, 2)),
            dma((peers, 2)),
            dma((X,)),
            dma((X,)),
            dma((NY, Y)),
            dma((NY, Y)),
            dma((NY, ZH)),
            dma((NY, ZH)),
            dma((NZ, ZH)),
            dma((NZ, ZH)),
            dma((NZ, Y)),
            dma((NZ, Y)),
            dma((Y,)),
            dma((Y,)),
            dma((ZH,)),
            dma((ZH,)),
        ],
        compiler_params=pltpu.CompilerParams(
            collective_id=0, has_side_effects=True, vmem_limit_bytes=56 << 20
        ),
    )(
        codes,
        exponents.reshape(1, rows),
        centroids.reshape(X, slice_rows, width),
        counters.reshape(cells // 128, 128),
    )
    return sums[None], mass


def solution(mesh):
    in_specs = (P(("pts", "cells"), None), P(("pts", "cells")), P("cells", None), P("cells"))
    out_specs = (P("cells", "pts", None), P("cells", "pts"))
    return jax.shard_map(body, mesh=mesh, in_specs=in_specs, out_specs=out_specs, check_vma=False)
```

```python
import functools
import math

import jax
import jax.numpy as jnp
from jax import lax
from jax.experimental import pallas as pl
from jax.experimental.pallas import tpu as pltpu
from jax.sharding import PartitionSpec as P

X, Y, ZH, ZL, CORES = 4, 8, 3, 4, 2
HALVES, QUARTERS = 2, 4
Y_PIECES = (((0, 2), (0, 1)), ((0, 2), (1, 2)), ((0, 1), (2, 3)))
Z_PIECES = (((0, 2), (3, 4)), ((1, 2), (2, 3)))
NY, NZ = len(Y_PIECES), len(Z_PIECES)
MESH = pl.DeviceIdType.MESH
F32, BF16 = jnp.float32, jnp.bfloat16


def power_of_minus(e):
    value = jnp.ones(e.shape, F32)
    for bit in range(7):
        step = jnp.full(e.shape, 2.0 ** -(2**bit), F32)
        value = value * jnp.where(((e >> bit) & 1) == 1, step, 1.0)
    return value


def dot_nt(a, b):
    return lax.dot_general(a, b, (((1,), (1,)), ((), ())), preferred_element_type=F32)


def kernel(
    scale,
    codes_hbm, exps_hbm, cent_hbm, counters_hbm,
    sums_ref, mass_ref,
    codes, exps, cent, counters, pts, inv, tmp, logit, share, acc, massacc,
    stats, rm, y_out, y_in, y_sum, yz_out, yz_in, z_out, z_in, z_sum, zy_out, zy_in,
    m_out, my_in, mz_out, mz_in,
    load_sem, g_send, g_recv, s_send, s_recv, r_send, r_recv,
    y_send, y_recv, yz_send, yz_recv, z_send, z_recv, zy_send, zy_recv,
    my_send, my_recv, mz_send, mz_recv,
):
    p = lax.axis_index("pts")
    me = lax.axis_index("cells")
    x = lax.div(p, Y * ZH)
    y = lax.rem(lax.div(p, ZH), Y)
    zh = lax.rem(p, ZH)
    zl = lax.div(me, CORES)
    core = lax.rem(me, CORES)
    other = 1 - core
    peers = ZL * CORES
    half_chips = ZL // 2
    half = lax.div(zl, half_chips)
    rows, width = pts.shape[3:]
    line = ZL * CORES * rows
    lanes = line // 2
    slice_rows = cent.shape[1]
    z_rows = acc.shape[2]

    def cut(piece):
        high, wide = z_rows // HALVES, width // QUARTERS
        (r0, r1), (c0, c1) = piece
        return slice(r0 * high, r1 * high), slice(c0 * wide, c1 * wide)

    y_cuts = [cut(piece) for piece in Y_PIECES]
    z_cuts = [cut(piece) for piece in Z_PIECES]

    def at_x(j):
        return ((lax.rem(x + j, X) * Y + y) * ZH + zh, me)

    def at_y(k):
        return ((x * Y + lax.rem(y + k, Y)) * ZH + zh, me)

    def at_z(k):
        return ((x * Y + y) * ZH + lax.rem(zh + k, ZH), me)

    def at_cells(k):
        return (p, lax.rem(me + k, peers))

    sibling = (p, zl * CORES + other)

    def send(src, dst, send_sem, recv_sem, device):
        return pltpu.make_async_remote_copy(
            src_ref=src, dst_ref=dst, send_sem=send_sem, recv_sem=recv_sem,
            device_id=device, device_id_type=MESH,
        )

    loads = [
        pltpu.make_async_copy(src, dst, load_sem.at[i])
        for i, (src, dst) in enumerate(
            ((exps_hbm, exps), (codes_hbm, codes), (counters_hbm, counters), (cent_hbm, cent))
        )
    ]
    for load in loads:
        load.start()

    barrier = pltpu.get_barrier_semaphore()

    def greet(device):
        pl.semaphore_signal(barrier, inc=1, device_id=device, device_id_type=MESH)

    for k in range(1, peers):
        greet(at_cells(k))
    for j in range(1, X):
        greet(at_x(j))
    for k in range(1, ZH):
        greet(at_z(k))
    for k in range(1, Y):
        greet(at_y(k))

    n_exp = exps.shape[1]
    diagonal = lax.broadcasted_iota(jnp.int32, (n_exp, n_exp), 0) == lax.broadcasted_iota(
        jnp.int32, (n_exp, n_exp), 1
    )
    loads[0].wait()
    powers = power_of_minus(exps[...])
    column = jnp.sum(jnp.where(diagonal, powers, 0.0), axis=1, keepdims=True)
    loads[1].wait()
    pts[x, zl, core] = (codes[...].astype(F32) * column).astype(BF16)

    pl.semaphore_wait(barrier, (Y - 1) + (ZH - 1) + (peers - 1) + (X - 1))

    def block(xx, zz, cc, device, sem):
        ref = pts.at[xx, zz, cc]
        return send(ref, ref, g_send.at[sem], g_recv.at[xx, zz, cc], device)

    for k in range(1, ZL):
        block(x, zl, core, (p, lax.rem(zl + k, ZL) * CORES + core), k).start()
    block(x, zl, core, sibling, 0).start()
    for j in range(1, X):
        block(x, zl, core, at_x(j), ZL - 1 + j).start()
    sem_zl = ZL + X - 1
    sem_x = sem_zl + (ZL - 1) * X

    square = (128, 128)
    eye = lax.broadcasted_iota(jnp.int32, square, 0) == lax.broadcasted_iota(jnp.int32, square, 1)
    loads[2].wait()

    def spread(g, carry):
        row = lax.rsqrt(counters[pl.ds(g, 1), :].astype(F32) + 1.0)
        col = jnp.sum(jnp.where(eye, row, 0.0), axis=1, keepdims=True)
        inv[pl.ds(pl.multiple_of(g * 128, 128), 128), :] = jnp.broadcast_to(col, square)
        return carry

    lax.fori_loop(0, counters.shape[0], spread, 0)
    loads[3].wait()

    def stat_copy(src, hh, k):
        ref = stats.at[src, hh]
        return send(ref, ref, s_send.at[k, hh], s_recv.at[src, hh], at_cells(k))

    def points_of(xx, hh):
        return pts[xx, pl.ds(hh * half_chips, half_chips)].reshape(lanes, width)

    def local_stats(hh):
        points = points_of(x, hh)

        def product(s, top):
            part = dot_nt(cent[s], points)
            tmp[s] = part
            return jnp.maximum(top, jnp.max(part, axis=0, keepdims=True))

        top = lax.fori_loop(0, X, product, jnp.full((1, lanes), -jnp.inf, F32))
        shift = top * scale

        def add_up(s, sums):
            expo = jnp.exp2(tmp[s] * scale - shift)
            weights = inv[pl.ds(pl.multiple_of(s * slice_rows, 128), slice_rows), :]
            weights = jnp.concatenate([weights] * (lanes // 128), axis=1)
            return (
                sums[0] + jnp.sum(expo, axis=0, keepdims=True),
                sums[1] + jnp.sum(expo * weights, axis=0, keepdims=True),
            )

        zero = jnp.zeros((1, lanes), F32)
        total, novel = lax.fori_loop(0, X, add_up, (zero, zero))
        stats[me, hh, 0:1, :] = top
        stats[me, hh, 1:2, :] = total
        stats[me, hh, 2:3, :] = novel

        def start(k, carry):
            stat_copy(me, hh, k).start()
            return carry

        lax.fori_loop(1, peers, start, 0)
        logit[x, :, pl.ds(pl.multiple_of(hh * lanes, 128), lanes)] = tmp[x]

    def forward(zz, slot):
        block(x, zz, core, sibling, 0).wait_recv()
        for j in range(1, X):
            block(x, zz, core, at_x(j), sem_zl + slot * X + j).start()
        block(x, zz, core, sibling, sem_zl + slot * X).start()

    begin = half * half_chips
    for k in range(1, half_chips):
        forward(begin + lax.rem(zl - begin + k, half_chips), k - 1)
    for k in range(half_chips):
        block(x, begin + k, other, sibling, 0).wait_recv()
    local_stats(half)
    begin = (1 - half) * half_chips
    for k in range(half_chips):
        forward(begin + k, half_chips - 1 + k)
    for k in range(half_chips):
        block(x, begin + k, other, sibling, 0).wait_recv()
    local_stats(1 - half)

    x_order = [1, 3, 2] if X == 4 else list(range(1, X))

    def pass_on(hh):
        for i, j in enumerate(x_order):
            xx = lax.rem(x + j, X)
            for k in range(half_chips):
                zz = hh * half_chips + k
                block(xx, zz, core, sibling, 0).wait_recv()
                block(xx, zz, core, sibling, sem_x + i * ZL + zz).start()

    def x_logits(j):
        xx = lax.rem(x + j, X)
        for zz in range(ZL):
            block(xx, zz, other, sibling, 0).wait_recv()
        logit[xx] = dot_nt(cent[x], pts[xx].reshape(line, width))

    pass_on(half)

    def stats_in(k, carry):
        src = lax.rem(me + k, peers)
        for hh in range(2):
            stat_copy(src, hh, k).wait_recv()
        return carry

    lax.fori_loop(1, peers, stats_in, 0)
    for hh in range(2):
        here = slice(hh * lanes, (hh + 1) * lanes)
        tops = stats[:, hh, 0, :]
        top = jnp.max(tops, axis=0, keepdims=True)
        ratio = jnp.exp2((tops - top) * scale)
        total = jnp.sum(stats[:, hh, 1, :] * ratio, axis=0, keepdims=True)
        novel = jnp.sum(stats[:, hh, 2, :] * ratio, axis=0, keepdims=True)
        rm[x, 0:1, here] = top * scale
        rm[x, 1:2, here] = novel / total / total

    def rm_copy(src, j):
        return send(rm.at[src], rm.at[src], r_send.at[j], r_recv.at[src], at_x(j))

    for j in range(1, X):
        rm_copy(x, j).start()

    acc[...] = jnp.zeros(acc.shape, F32)
    massacc[...] = jnp.zeros(massacc.shape, F32)

    def accumulate(xx):
        for q in range(line // 128):
            here = slice(q * 128, (q + 1) * 128)
            shift, factor = rm[xx, 0:1, here], rm[xx, 1:2, here]
            part = (jnp.exp2(logit[xx, :, here] * scale - shift) * factor).astype(BF16)
            share[:, here] = part
            massacc[...] += part.astype(F32)
        acc[...] += jnp.dot(
            share[...], pts[xx].reshape(line, width), preferred_element_type=F32
        ).reshape(acc.shape)

    pass_on(1 - half)
    accumulate(x)
    for j in x_order:
        x_logits(j)
    for j in x_order:
        xx = lax.rem(x + j, X)
        rm_copy(xx, j).wait_recv()
        accumulate(xx)

    def y_copy(q, src, k, dst):
        return send(y_out[q].at[dst], y_in[q].at[src], y_send.at[q, k], y_recv.at[q, src], at_y(k))

    def z_copy(q, src, k, dst):
        return send(z_out[q].at[dst], z_in[q].at[src], z_send.at[q, k], z_recv.at[q, src], at_z(k))

    def yz_copy(q, src, k, dst):
        return send(
            yz_out[q].at[dst], yz_in[q].at[src], yz_send.at[q, k], yz_recv.at[q, src], at_z(k)
        )

    def zy_copy(q, src, k, dst):
        return send(
            zy_out[q].at[dst], zy_in[q].at[src], zy_send.at[q, k], zy_recv.at[q, src], at_y(k)
        )

    def my_copy(src, k):
        return send(m_out, my_in.at[src], my_send.at[k], my_recv.at[src], at_y(k))

    def mz_copy(src, k):
        return send(mz_out, mz_in.at[src], mz_send.at[k], mz_recv.at[src], at_z(k))

    def over_y(step, first=0):
        return lax.fori_loop(1, Y, step, first)

    def over_z(step, first=0):
        return lax.fori_loop(1, ZH, step, first)

    def y_first(q):
        def start(k, carry):
            dst = lax.rem(y + k, Y)
            y_out[q][dst] = acc[dst, :, *y_cuts[q]].astype(BF16)
            y_copy(q, y, k, dst).start()
            return carry

        over_y(start)

    def z_first(q):
        def start(k, carry):
            dst = lax.rem(zh + k, ZH)
            z_out[q][dst] = acc[:, dst, *z_cuts[q]].astype(BF16)
            z_copy(q, zh, k, dst).start()
            return carry

        over_z(start)

    def y_then_z(q):
        def add(k, total):
            src = lax.rem(y + k, Y)
            y_copy(q, src, k, src).wait_recv()
            return total + y_in[q][src].astype(F32)

        y_sum[q][...] = over_y(add, acc[y, :, *y_cuts[q]])

        def start(k, carry):
            dst = lax.rem(zh + k, ZH)
            yz_out[q][dst] = y_sum[q][dst].astype(BF16)
            yz_copy(q, zh, k, dst).start()
            return carry

        over_z(start)

    def z_then_y(q):
        def add(k, carry):
            src = lax.rem(zh + k, ZH)
            z_copy(q, src, k, src).wait_recv()
            z_sum[q][...] += z_in[q][src].astype(F32)
            return carry

        z_sum[q][...] = acc[:, zh, *z_cuts[q]]
        over_z(add)

        def start(k, carry):
            dst = lax.rem(y + k, Y)
            zy_out[q][dst] = z_sum[q][dst].astype(BF16)
            zy_copy(q, y, k, dst).start()
            return carry

        over_y(start)

    def finish_y(q):
        def add(k, total):
            src = lax.rem(zh + k, ZH)
            yz_copy(q, src, k, src).wait_recv()
            return total + yz_in[q][src].astype(F32)

        sums_ref[*y_cuts[q]] = over_z(add, y_sum[q][zh])

    def finish_z(q):
        def add(k, total):
            src = lax.rem(y + k, Y)
            zy_copy(q, src, k, src).wait_recv()
            return total + zy_in[q][src].astype(F32)

        sums_ref[*z_cuts[q]] = over_y(add, z_sum[q][y])

    for q in range(max(NY, NZ)):
        if q < NY:
            y_first(q)
        if q < NZ:
            z_first(q)

    m_out[...] = jnp.zeros(m_out.shape, F32)
    for g in range(slice_rows // 128):
        col = jnp.sum(massacc[g * 128 : (g + 1) * 128, :], axis=1, keepdims=True)
        m_out[g : g + 1, :] = jnp.sum(jnp.where(eye, col, 0.0), axis=0, keepdims=True)

    def my_start(k, carry):
        my_copy(y, k).start()
        return carry

    over_y(my_start)

    for q in range(max(NY, NZ)):
        if q < NY:
            y_then_z(q)
        if q < NZ:
            z_then_y(q)
        if q == 0:

            def my_add(k, total):
                src = lax.rem(y + k, Y)
                my_copy(src, k).wait_recv()
                return total + my_in[src]

            mass = over_y(my_add, m_out[...])
            mz_out[...] = mass

            def mz_start(k, carry):
                mz_copy(zh, k).start()
                return carry

            over_z(mz_start)

    def mz_add(k, total):
        src = lax.rem(zh + k, ZH)
        mz_copy(src, k).wait_recv()
        return total + mz_in[src]

    mass = over_z(mz_add, mass)
    per_row = 128 // z_rows
    place = y * ZH + zh
    at_line = lax.broadcasted_iota(jnp.int32, mass.shape, 0) == lax.div(place, per_row)
    picked = jnp.sum(jnp.where(at_line, mass, 0.0), axis=0, keepdims=True)
    which = lax.rem(place, per_row)
    answer = jnp.zeros((1, z_rows), F32)
    for q in range(per_row):
        answer = jnp.where(which == q, picked[:, q * z_rows : (q + 1) * z_rows], answer)
    mass_ref[...] = answer

    for q in range(max(NY, NZ)):
        if q < NY:
            finish_y(q)
        if q < NZ:
            finish_z(q)

    def sent_block(i, carry):
        block(x, zl, core, sibling, i).wait_send()
        return carry

    lax.fori_loop(0, g_send.shape[0], sent_block, 0)

    def sent_stats(k, carry):
        for hh in range(2):
            stat_copy(me, hh, k).wait_send()
        return carry

    lax.fori_loop(1, peers, sent_stats, 0)
    for j in range(1, X):
        rm_copy(x, j).wait_send()

    def sent_y(k, carry):
        dst = lax.rem(y + k, Y)
        for q in range(NY):
            y_copy(q, y, k, dst).wait_send()
        for q in range(NZ):
            zy_copy(q, y, k, dst).wait_send()
        my_copy(y, k).wait_send()
        return carry

    over_y(sent_y)

    def sent_z(k, carry):
        dst = lax.rem(zh + k, ZH)
        for q in range(NY):
            yz_copy(q, zh, k, dst).wait_send()
        for q in range(NZ):
            z_copy(q, zh, k, dst).wait_send()
        mz_copy(zh, k).wait_send()
        return carry

    over_z(sent_z)


def body(codes, exponents, centroids, counters):
    rows, width = codes.shape
    cells = centroids.shape[0]
    slice_rows = cells // X
    z_rows = slice_rows // Y // ZH
    line = ZL * CORES * rows
    lanes = line // 2
    peers = ZL * CORES

    def size(piece):
        (r0, r1), (c0, c1) = piece
        return (r1 - r0) * z_rows // HALVES, (c1 - c0) * width // QUARTERS

    y_sizes = [size(piece) for piece in Y_PIECES]
    z_sizes = [size(piece) for piece in Z_PIECES]
    scale = 4.0 / math.sqrt(width) * math.log2(math.e)
    vmem, dma = pltpu.VMEM, pltpu.SemaphoreType.DMA
    hbm = pl.BlockSpec(memory_space=pltpu.HBM)
    sums, mass = pl.pallas_call(
        functools.partial(kernel, scale),
        out_shape=(
            jax.ShapeDtypeStruct((z_rows, width), F32),
            jax.ShapeDtypeStruct((1, z_rows), F32),
        ),
        in_specs=[hbm] * 4,
        out_specs=(pl.BlockSpec(memory_space=vmem), pl.BlockSpec(memory_space=vmem)),
        scratch_shapes=[
            vmem((rows, width), jnp.int32),
            vmem((1, rows), jnp.int32),
            vmem((X, slice_rows, width), BF16),
            vmem((cells // 128, 128), jnp.int32),
            vmem((X, ZL, CORES, rows, width), BF16),
            vmem((cells, 128), F32),
            vmem((X, slice_rows, lanes), F32),
            vmem((X, slice_rows, line), F32),
            vmem((slice_rows, line), BF16),
            vmem((Y, ZH, z_rows, width), F32),
            vmem((slice_rows, 128), F32),
            vmem((peers, 2, 8, lanes), F32),
            vmem((X, 8, line), F32),
            [vmem((Y, ZH, *size), BF16) for size in y_sizes],
            [vmem((Y, ZH, *size), BF16) for size in y_sizes],
            [vmem((ZH, *size), F32) for size in y_sizes],
            [vmem((ZH, *size), BF16) for size in y_sizes],
            [vmem((ZH, *size), BF16) for size in y_sizes],
            [vmem((ZH, Y, *size), BF16) for size in z_sizes],
            [vmem((ZH, Y, *size), BF16) for size in z_sizes],
            [vmem((Y, *size), F32) for size in z_sizes],
            [vmem((Y, *size), BF16) for size in z_sizes],
            [vmem((Y, *size), BF16) for size in z_sizes],
            vmem((8, 128), F32),
            vmem((Y, 8, 128), F32),
            vmem((8, 128), F32),
            vmem((ZH, 8, 128), F32),
            dma((4,)),
            dma((X + ZL - 1 + (ZL - 1) * X + (X - 1) * ZL,)),
            dma((X, ZL, CORES)),
            dma((peers, 2)),
            dma((peers, 2)),
            dma((X,)),
            dma((X,)),
            dma((NY, Y)),
            dma((NY, Y)),
            dma((NY, ZH)),
            dma((NY, ZH)),
            dma((NZ, ZH)),
            dma((NZ, ZH)),
            dma((NZ, Y)),
            dma((NZ, Y)),
            dma((Y,)),
            dma((Y,)),
            dma((ZH,)),
            dma((ZH,)),
        ],
        compiler_params=pltpu.CompilerParams(
            collective_id=0, has_side_effects=True, vmem_limit_bytes=48 << 20
        ),
    )(*(
        pltpu.with_memory_space_constraint(a, pltpu.HBM)
        for a in (
            codes,
            exponents.reshape(1, rows),
            centroids.reshape(X, slice_rows, width),
            counters.reshape(cells // 128, 128),
        )
    ))
    return sums[None], mass


def solution(mesh):
    in_specs = (P(("pts", "cells"), None), P(("pts", "cells")), P("cells", None), P("cells"))
    out_specs = (P("cells", "pts", None), P("cells", "pts"))
    return jax.shard_map(body, mesh=mesh, in_specs=in_specs, out_specs=out_specs, check_vma=False)
```

```python
import functools
import math

import jax
import jax.numpy as jnp
from jax import lax
from jax.experimental import pallas as pl
from jax.experimental.pallas import tpu as pltpu
from jax.sharding import PartitionSpec as P

X, Y, ZH, ZL, CORES = 4, 8, 3, 4, 2
HALVES, QUARTERS = 2, 4
Y_PIECES = (((0, 2), (0, 2)), ((0, 1), (2, 3)))
Z_PIECES = (((0, 2), (3, 4)), ((1, 2), (2, 3)))
NY, NZ = len(Y_PIECES), len(Z_PIECES)
MESH = pl.DeviceIdType.MESH
F32, BF16 = jnp.float32, jnp.bfloat16


def power_of_minus(e):
    value = jnp.ones(e.shape, F32)
    for bit in range(7):
        step = jnp.full(e.shape, 2.0 ** -(2**bit), F32)
        value = value * jnp.where(((e >> bit) & 1) == 1, step, 1.0)
    return value


def dot_nt(a, b):
    return lax.dot_general(a, b, (((1,), (1,)), ((), ())), preferred_element_type=F32)


def kernel(
    scale,
    codes_hbm, exps_hbm, cent_hbm, counters_hbm,
    sums_ref, mass_ref,
    codes, exps, cent, counters, pts, inv, tmp, logit, share, acc, massacc,
    stats, rm, y_out, y_in, y_sum, yz_out, yz_in, z_out, z_in, z_sum, zy_out, zy_in,
    m_out, my_in, mz_out, mz_in,
    load_sem, g_send, g_recv, s_send, s_recv, r_send, r_recv,
    y_send, y_recv, yz_send, yz_recv, z_send, z_recv, zy_send, zy_recv,
    my_send, my_recv, mz_send, mz_recv,
):
    p = lax.axis_index("pts")
    me = lax.axis_index("cells")
    x = lax.div(p, Y * ZH)
    y = lax.rem(lax.div(p, ZH), Y)
    zh = lax.rem(p, ZH)
    zl = lax.div(me, CORES)
    core = lax.rem(me, CORES)
    other = 1 - core
    peers = ZL * CORES
    half_chips = ZL // 2
    half = lax.div(zl, half_chips)
    rows, width = pts.shape[3:]
    line = ZL * CORES * rows
    lanes = line // 2
    slice_rows = cent.shape[1]
    z_rows = acc.shape[2]

    def cut(piece):
        high, wide = z_rows // HALVES, width // QUARTERS
        (r0, r1), (c0, c1) = piece
        return slice(r0 * high, r1 * high), slice(c0 * wide, c1 * wide)

    y_cuts = [cut(piece) for piece in Y_PIECES]
    z_cuts = [cut(piece) for piece in Z_PIECES]

    def at_x(j):
        return ((lax.rem(x + j, X) * Y + y) * ZH + zh, me)

    def at_y(k):
        return ((x * Y + lax.rem(y + k, Y)) * ZH + zh, me)

    def at_z(k):
        return ((x * Y + y) * ZH + lax.rem(zh + k, ZH), me)

    def at_cells(k):
        return (p, lax.rem(me + k, peers))

    sibling = (p, zl * CORES + other)

    def send(src, dst, send_sem, recv_sem, device):
        return pltpu.make_async_remote_copy(
            src_ref=src, dst_ref=dst, send_sem=send_sem, recv_sem=recv_sem,
            device_id=device, device_id_type=MESH,
        )

    loads = [
        pltpu.make_async_copy(src, dst, load_sem.at[i])
        for i, (src, dst) in enumerate(
            ((exps_hbm, exps), (codes_hbm, codes), (counters_hbm, counters), (cent_hbm, cent))
        )
    ]
    for load in loads[:2]:
        load.start()

    barrier = pltpu.get_barrier_semaphore()

    def greet(device):
        pl.semaphore_signal(barrier, inc=1, device_id=device, device_id_type=MESH)

    for k in sorted(range(1, Y), key=lambda k: -min(k, Y - k)):
        greet(at_y(k))
    for k in range(1, ZH):
        greet(at_z(k))
    for k in range(1, peers):
        greet(at_cells(k))
    for j in range(1, X):
        greet(at_x(j))

    for load in loads[2:]:
        load.start()

    n_exp = exps.shape[1]
    diagonal = lax.broadcasted_iota(jnp.int32, (n_exp, n_exp), 0) == lax.broadcasted_iota(
        jnp.int32, (n_exp, n_exp), 1
    )
    loads[0].wait()
    powers = power_of_minus(exps[...])
    column = jnp.sum(jnp.where(diagonal, powers, 0.0), axis=1, keepdims=True)
    loads[1].wait()
    pts[x, zl, core] = (codes[...].astype(F32) * column).astype(BF16)

    pl.semaphore_wait(barrier, (Y - 1) + (ZH - 1) + (peers - 1) + (X - 1))

    def block(xx, zz, cc, device, sem):
        ref = pts.at[xx, zz, cc]
        return send(ref, ref, g_send.at[sem], g_recv.at[xx, zz, cc], device)

    for k in range(1, ZL):
        block(x, zl, core, (p, lax.rem(zl + k, ZL) * CORES + core), k).start()
    block(x, zl, core, sibling, 0).start()
    for j in range(1, X):
        block(x, zl, core, at_x(j), ZL - 1 + j).start()
    sem_zl = ZL + X - 1
    sem_x = sem_zl + (ZL - 1) * X

    square = (128, 128)
    eye = lax.broadcasted_iota(jnp.int32, square, 0) == lax.broadcasted_iota(jnp.int32, square, 1)
    loads[2].wait()

    def spread(g, carry):
        row = lax.rsqrt(counters[pl.ds(g, 1), :].astype(F32) + 1.0)
        col = jnp.sum(jnp.where(eye, row, 0.0), axis=1, keepdims=True)
        inv[pl.ds(pl.multiple_of(g * 128, 128), 128), :] = jnp.broadcast_to(col, square)
        return carry

    lax.fori_loop(0, counters.shape[0], spread, 0)
    loads[3].wait()

    def stat_copy(src, hh, k):
        ref = stats.at[src, hh]
        return send(ref, ref, s_send.at[k, hh], s_recv.at[src, hh], at_cells(k))

    def points_of(xx, hh):
        return pts[xx, pl.ds(hh * half_chips, half_chips)].reshape(lanes, width)

    def local_stats(hh):
        points = points_of(x, hh)

        def product(s, top):
            part = dot_nt(cent[s], points)
            tmp[s] = part
            return jnp.maximum(top, jnp.max(part, axis=0, keepdims=True))

        top = lax.fori_loop(0, X, product, jnp.full((1, lanes), -jnp.inf, F32))
        shift = top * scale

        def add_up(s, sums):
            expo = jnp.exp2(tmp[s] * scale - shift)
            weights = inv[pl.ds(pl.multiple_of(s * slice_rows, 128), slice_rows), :]
            weights = jnp.concatenate([weights] * (lanes // 128), axis=1)
            return (
                sums[0] + jnp.sum(expo, axis=0, keepdims=True),
                sums[1] + jnp.sum(expo * weights, axis=0, keepdims=True),
            )

        zero = jnp.zeros((1, lanes), F32)
        total, novel = lax.fori_loop(0, X, add_up, (zero, zero))
        stats[me, hh, 0:1, :] = top
        stats[me, hh, 1:2, :] = total
        stats[me, hh, 2:3, :] = novel

        def start(k, carry):
            stat_copy(me, hh, k).start()
            return carry

        lax.fori_loop(1, peers, start, 0)
        logit[x, :, pl.ds(pl.multiple_of(hh * lanes, 128), lanes)] = tmp[x]

    def forward(zz, slot):
        block(x, zz, core, sibling, 0).wait_recv()
        block(x, zz, core, sibling, sem_zl + slot * X).start()
        for j in range(1, X):
            block(x, zz, core, at_x(j), sem_zl + slot * X + j).start()

    begin = half * half_chips
    for k in range(1, half_chips):
        forward(begin + lax.rem(zl - begin + k, half_chips), k - 1)
    for k in range(half_chips):
        block(x, begin + k, other, sibling, 0).wait_recv()
    local_stats(half)
    begin = (1 - half) * half_chips
    for k in range(half_chips):
        forward(begin + k, half_chips - 1 + k)
    for k in range(half_chips):
        block(x, begin + k, other, sibling, 0).wait_recv()
    local_stats(1 - half)

    x_order = [1, 3, 2] if X == 4 else list(range(1, X))

    def pass_on(hh):
        for i, j in enumerate(x_order):
            xx = lax.rem(x + j, X)
            for k in range(half_chips):
                zz = hh * half_chips + k
                block(xx, zz, core, sibling, 0).wait_recv()
                block(xx, zz, core, sibling, sem_x + i * ZL + zz).start()

    def x_logits(j):
        xx = lax.rem(x + j, X)
        for zz in range(ZL):
            block(xx, zz, other, sibling, 0).wait_recv()
        logit[xx] = dot_nt(cent[x], pts[xx].reshape(line, width))

    pass_on(half)

    def stats_in(k, carry):
        src = lax.rem(me + k, peers)
        for hh in range(2):
            stat_copy(src, hh, k).wait_recv()
        return carry

    lax.fori_loop(1, peers, stats_in, 0)
    for hh in range(2):
        here = slice(hh * lanes, (hh + 1) * lanes)
        tops = stats[:, hh, 0, :]
        top = jnp.max(tops, axis=0, keepdims=True)
        ratio = jnp.exp2((tops - top) * scale)
        total = jnp.sum(stats[:, hh, 1, :] * ratio, axis=0, keepdims=True)
        novel = jnp.sum(stats[:, hh, 2, :] * ratio, axis=0, keepdims=True)
        rm[x, 0:1, here] = top * scale
        rm[x, 1:2, here] = novel / total / total

    def rm_copy(src, j):
        return send(rm.at[src], rm.at[src], r_send.at[j], r_recv.at[src], at_x(j))

    for j in range(1, X):
        rm_copy(x, j).start()

    acc[...] = jnp.zeros(acc.shape, F32)
    massacc[...] = jnp.zeros(massacc.shape, F32)

    def weigh(xx, slot):
        for q in range(line // 128):
            here = slice(q * 128, (q + 1) * 128)
            shift, factor = rm[xx, 0:1, here], rm[xx, 1:2, here]
            part = (jnp.exp2(logit[xx, :, here] * scale - shift) * factor).astype(BF16)
            share[slot][:, here] = part
            massacc[...] += part.astype(F32)

    def add_product(xx, slot):
        acc[...] += jnp.dot(
            share[slot][...], pts[xx].reshape(line, width), preferred_element_type=F32
        ).reshape(acc.shape)

    pass_on(1 - half)
    weigh(x, 0)
    add_product(x, 0)
    for j in x_order:
        x_logits(j)
    for j in x_order:
        rm_copy(lax.rem(x + j, X), j).wait_recv()
    for i, j in enumerate(x_order):
        weigh(lax.rem(x + j, X), i)
        if i > 0:
            add_product(lax.rem(x + x_order[i - 1], X), i - 1)
    add_product(lax.rem(x + x_order[-1], X), len(x_order) - 1)

    def y_copy(q, src, k, dst):
        return send(y_out[q].at[dst], y_in[q].at[src], y_send.at[q, k], y_recv.at[q, src], at_y(k))

    def z_copy(q, src, k, dst):
        return send(z_out[q].at[dst], z_in[q].at[src], z_send.at[q, k], z_recv.at[q, src], at_z(k))

    def yz_copy(q, src, k, dst):
        return send(
            yz_out[q].at[dst], yz_in[q].at[src], yz_send.at[q, k], yz_recv.at[q, src], at_z(k)
        )

    def zy_copy(q, src, k, dst):
        return send(
            zy_out[q].at[dst], zy_in[q].at[src], zy_send.at[q, k], zy_recv.at[q, src], at_y(k)
        )

    def my_copy(src, k):
        return send(m_out, my_in.at[src], my_send.at[k], my_recv.at[src], at_y(k))

    def mz_copy(src, k):
        return send(mz_out, mz_in.at[src], mz_send.at[k], mz_recv.at[src], at_z(k))

    def over_y(step, first=0):
        return lax.fori_loop(1, Y, step, first)

    def over_z(step, first=0):
        return lax.fori_loop(1, ZH, step, first)

    def y_first(q):
        def start(k, carry):
            dst = lax.rem(y + k, Y)
            y_out[q][dst] = acc[dst, :, *y_cuts[q]].astype(BF16)
            y_copy(q, y, k, dst).start()
            return carry

        over_y(start)

    def z_first(q):
        def start(k, carry):
            dst = lax.rem(zh + k, ZH)
            z_out[q][dst] = acc[:, dst, *z_cuts[q]].astype(BF16)
            z_copy(q, zh, k, dst).start()
            return carry

        over_z(start)

    def y_then_z(q):
        def add(k, total):
            src = lax.rem(y + k, Y)
            y_copy(q, src, k, src).wait_recv()
            return total + y_in[q][src].astype(F32)

        y_sum[q][...] = over_y(add, acc[y, :, *y_cuts[q]])

        def start(k, carry):
            dst = lax.rem(zh + k, ZH)
            yz_out[q][dst] = y_sum[q][dst].astype(BF16)
            yz_copy(q, zh, k, dst).start()
            return carry

        over_z(start)

    def z_then_y(q):
        def add(k, carry):
            src = lax.rem(zh + k, ZH)
            z_copy(q, src, k, src).wait_recv()
            z_sum[q][...] += z_in[q][src].astype(F32)
            return carry

        z_sum[q][...] = acc[:, zh, *z_cuts[q]]
        over_z(add)

        def start(k, carry):
            dst = lax.rem(y + k, Y)
            zy_out[q][dst] = z_sum[q][dst].astype(BF16)
            zy_copy(q, y, k, dst).start()
            return carry

        over_y(start)

    def finish_y(q):
        def add(k, total):
            src = lax.rem(zh + k, ZH)
            yz_copy(q, src, k, src).wait_recv()
            return total + yz_in[q][src].astype(F32)

        sums_ref[*y_cuts[q]] = over_z(add, y_sum[q][zh])

    def finish_z(q):
        def add(k, total):
            src = lax.rem(y + k, Y)
            zy_copy(q, src, k, src).wait_recv()
            return total + zy_in[q][src].astype(F32)

        sums_ref[*z_cuts[q]] = over_y(add, z_sum[q][y])

    for q in range(max(NY, NZ)):
        if q < NZ:
            z_first(q)
        if q < NY:
            y_first(q)

    m_out[...] = jnp.zeros(m_out.shape, F32)
    for g in range(slice_rows // 128):
        col = jnp.sum(massacc[g * 128 : (g + 1) * 128, :], axis=1, keepdims=True)
        m_out[g : g + 1, :] = jnp.sum(jnp.where(eye, col, 0.0), axis=0, keepdims=True)

    def my_start(k, carry):
        my_copy(y, k).start()
        return carry

    over_y(my_start)

    for q in range(max(NY, NZ)):
        if q < NY:
            y_then_z(q)
        if q < NZ:
            z_then_y(q)
        if q == 0:

            def my_add(k, total):
                src = lax.rem(y + k, Y)
                my_copy(src, k).wait_recv()
                return total + my_in[src]

            mass = over_y(my_add, m_out[...])
            mz_out[...] = mass

            def mz_start(k, carry):
                mz_copy(zh, k).start()
                return carry

            over_z(mz_start)

    def mz_add(k, total):
        src = lax.rem(zh + k, ZH)
        mz_copy(src, k).wait_recv()
        return total + mz_in[src]

    mass = over_z(mz_add, mass)
    per_row = 128 // z_rows
    place = y * ZH + zh
    at_line = lax.broadcasted_iota(jnp.int32, mass.shape, 0) == lax.div(place, per_row)
    picked = jnp.sum(jnp.where(at_line, mass, 0.0), axis=0, keepdims=True)
    which = lax.rem(place, per_row)
    answer = jnp.zeros((1, z_rows), F32)
    for q in range(per_row):
        answer = jnp.where(which == q, picked[:, q * z_rows : (q + 1) * z_rows], answer)
    mass_ref[...] = answer

    for q in range(max(NY, NZ)):
        if q < NY:
            finish_y(q)
        if q < NZ:
            finish_z(q)

    def sent_block(i, carry):
        block(x, zl, core, sibling, i).wait_send()
        return carry

    lax.fori_loop(0, g_send.shape[0], sent_block, 0)

    def sent_stats(k, carry):
        for hh in range(2):
            stat_copy(me, hh, k).wait_send()
        return carry

    lax.fori_loop(1, peers, sent_stats, 0)
    for j in range(1, X):
        rm_copy(x, j).wait_send()

    def sent_y(k, carry):
        dst = lax.rem(y + k, Y)
        for q in range(NY):
            y_copy(q, y, k, dst).wait_send()
        for q in range(NZ):
            zy_copy(q, y, k, dst).wait_send()
        my_copy(y, k).wait_send()
        return carry

    over_y(sent_y)

    def sent_z(k, carry):
        dst = lax.rem(zh + k, ZH)
        for q in range(NY):
            yz_copy(q, zh, k, dst).wait_send()
        for q in range(NZ):
            z_copy(q, zh, k, dst).wait_send()
        mz_copy(zh, k).wait_send()
        return carry

    over_z(sent_z)


def body(codes, exponents, centroids, counters):
    rows, width = codes.shape
    cells = centroids.shape[0]
    slice_rows = cells // X
    z_rows = slice_rows // Y // ZH
    line = ZL * CORES * rows
    lanes = line // 2
    peers = ZL * CORES

    def size(piece):
        (r0, r1), (c0, c1) = piece
        return (r1 - r0) * z_rows // HALVES, (c1 - c0) * width // QUARTERS

    y_sizes = [size(piece) for piece in Y_PIECES]
    z_sizes = [size(piece) for piece in Z_PIECES]
    scale = 4.0 / math.sqrt(width) * math.log2(math.e)
    vmem, dma = pltpu.VMEM, pltpu.SemaphoreType.DMA
    hbm = pl.BlockSpec(memory_space=pltpu.HBM)
    sums, mass = pl.pallas_call(
        functools.partial(kernel, scale),
        out_shape=(
            jax.ShapeDtypeStruct((z_rows, width), F32),
            jax.ShapeDtypeStruct((1, z_rows), F32),
        ),
        in_specs=[hbm] * 4,
        out_specs=(pl.BlockSpec(memory_space=vmem), pl.BlockSpec(memory_space=vmem)),
        scratch_shapes=[
            vmem((rows, width), jnp.int32),
            vmem((1, rows), jnp.int32),
            vmem((X, slice_rows, width), BF16),
            vmem((cells // 128, 128), jnp.int32),
            vmem((X, ZL, CORES, rows, width), BF16),
            vmem((cells, 128), F32),
            vmem((X, slice_rows, lanes), F32),
            vmem((X, slice_rows, line), F32),
            [vmem((slice_rows, line), BF16) for _ in range(X - 1)],
            vmem((Y, ZH, z_rows, width), F32),
            vmem((slice_rows, 128), F32),
            vmem((peers, 2, 4, lanes), F32),
            vmem((X, 2, line), F32),
            [vmem((Y, ZH, *size), BF16) for size in y_sizes],
            [vmem((Y, ZH, *size), BF16) for size in y_sizes],
            [vmem((ZH, *size), F32) for size in y_sizes],
            [vmem((ZH, *size), BF16) for size in y_sizes],
            [vmem((ZH, *size), BF16) for size in y_sizes],
            [vmem((ZH, Y, *size), BF16) for size in z_sizes],
            [vmem((ZH, Y, *size), BF16) for size in z_sizes],
            [vmem((Y, *size), F32) for size in z_sizes],
            [vmem((Y, *size), BF16) for size in z_sizes],
            [vmem((Y, *size), BF16) for size in z_sizes],
            vmem((8, 128), F32),
            vmem((Y, 8, 128), F32),
            vmem((8, 128), F32),
            vmem((ZH, 8, 128), F32),
            dma((4,)),
            dma((X + ZL - 1 + (ZL - 1) * X + (X - 1) * ZL,)),
            dma((X, ZL, CORES)),
            dma((peers, 2)),
            dma((peers, 2)),
            dma((X,)),
            dma((X,)),
            dma((NY, Y)),
            dma((NY, Y)),
            dma((NY, ZH)),
            dma((NY, ZH)),
            dma((NZ, ZH)),
            dma((NZ, ZH)),
            dma((NZ, Y)),
            dma((NZ, Y)),
            dma((Y,)),
            dma((Y,)),
            dma((ZH,)),
            dma((ZH,)),
        ],
        compiler_params=pltpu.CompilerParams(
            collective_id=0, has_side_effects=True, vmem_limit_bytes=48 << 20
        ),
    )(*(
        pltpu.with_memory_space_constraint(a, pltpu.HBM)
        for a in (
            codes,
            exponents.reshape(1, rows),
            centroids.reshape(X, slice_rows, width),
            counters.reshape(cells // 128, 128),
        )
    ))
    return sums[None], mass


def solution(mesh):
    in_specs = (P(("pts", "cells"), None), P(("pts", "cells")), P("cells", None), P("cells"))
    out_specs = (P("cells", "pts", None), P("cells", "pts"))
    return jax.shard_map(body, mesh=mesh, in_specs=in_specs, out_specs=out_specs, check_vma=False)
```

```python
import functools
import math

import jax
import jax.numpy as jnp
from jax import lax
from jax.experimental import pallas as pl
from jax.experimental.pallas import tpu as pltpu
from jax.sharding import PartitionSpec as P

X, Y, ZH, ZL, CORES = 4, 8, 3, 4, 2
HALVES, QUARTERS = 2, 4
Y_PIECES = (((0, 2), (0, 2)), ((0, 1), (2, 3)))
Z_PIECES = (((0, 2), (3, 4)), ((1, 2), (2, 3)))
NY, NZ = len(Y_PIECES), len(Z_PIECES)
MESH = pl.DeviceIdType.MESH
F32, BF16 = jnp.float32, jnp.bfloat16


def power_of_minus(e):
    value = jnp.ones(e.shape, F32)
    for bit in range(7):
        step = jnp.full(e.shape, 2.0 ** -(2**bit), F32)
        value = value * jnp.where(((e >> bit) & 1) == 1, step, 1.0)
    return value


def dot_nt(a, b):
    return lax.dot_general(a, b, (((1,), (1,)), ((), ())), preferred_element_type=F32)


def kernel(
    scale,
    codes_hbm, exps_hbm, cent_hbm, counters_hbm,
    sums_ref, mass_ref,
    codes, exps, cent, counters, pts, inv, tmp, logit, share, acc, massacc,
    stats, rm, y_out, y_in, y_sum, yz_out, yz_in, z_out, z_in, z_sum, zy_out, zy_in,
    m_out, my_in, mz_out, mz_in,
    load_sem, g_send, g_recv, s_send, s_recv, r_send, r_recv,
    y_send, y_recv, yz_send, yz_recv, z_send, z_recv, zy_send, zy_recv,
    my_send, my_recv, mz_send, mz_recv,
):
    p = lax.axis_index("pts")
    me = lax.axis_index("cells")
    x = lax.div(p, Y * ZH)
    y = lax.rem(lax.div(p, ZH), Y)
    zh = lax.rem(p, ZH)
    zl = lax.div(me, CORES)
    core = lax.rem(me, CORES)
    other = 1 - core
    peers = ZL * CORES
    half_chips = ZL // 2
    half = lax.div(zl, half_chips)
    rows, width = pts.shape[3:]
    line = ZL * CORES * rows
    lanes = line // 2
    slice_rows = cent.shape[1]
    z_rows = acc.shape[2]

    def cut(piece):
        high, wide = z_rows // HALVES, width // QUARTERS
        (r0, r1), (c0, c1) = piece
        return slice(r0 * high, r1 * high), slice(c0 * wide, c1 * wide)

    y_cuts = [cut(piece) for piece in Y_PIECES]
    z_cuts = [cut(piece) for piece in Z_PIECES]

    def at_x(j):
        return ((lax.rem(x + j, X) * Y + y) * ZH + zh, me)

    def at_y(k):
        return ((x * Y + lax.rem(y + k, Y)) * ZH + zh, me)

    def at_z(k):
        return ((x * Y + y) * ZH + lax.rem(zh + k, ZH), me)

    def at_cells(k):
        return (p, lax.rem(me + k, peers))

    sibling = (p, zl * CORES + other)

    def send(src, dst, send_sem, recv_sem, device):
        return pltpu.make_async_remote_copy(
            src_ref=src, dst_ref=dst, send_sem=send_sem, recv_sem=recv_sem,
            device_id=device, device_id_type=MESH,
        )

    loads = [
        pltpu.make_async_copy(src, dst, load_sem.at[i])
        for i, (src, dst) in enumerate(
            ((exps_hbm, exps), (codes_hbm, codes), (counters_hbm, counters), (cent_hbm, cent))
        )
    ]
    for load in loads[:2]:
        load.start()

    barrier = pltpu.get_barrier_semaphore()

    def greet(device):
        pl.semaphore_signal(barrier, inc=1, device_id=device, device_id_type=MESH)

    for k in sorted(range(1, Y), key=lambda k: -min(k, Y - k)):
        greet(at_y(k))
    for k in range(1, ZH):
        greet(at_z(k))
    for k in range(1, peers):
        greet(at_cells(k))
    for j in range(1, X):
        greet(at_x(j))

    for load in loads[2:]:
        load.start()

    n_exp = exps.shape[1]
    diagonal = lax.broadcasted_iota(jnp.int32, (n_exp, n_exp), 0) == lax.broadcasted_iota(
        jnp.int32, (n_exp, n_exp), 1
    )
    loads[0].wait()
    powers = power_of_minus(exps[...])
    column = jnp.sum(jnp.where(diagonal, powers, 0.0), axis=1, keepdims=True)
    loads[1].wait()
    pts[x, zl, core] = (codes[...].astype(F32) * column).astype(BF16)

    pl.semaphore_wait(barrier, (Y - 1) + (ZH - 1) + (peers - 1) + (X - 1))

    def block(xx, zz, cc, device, sem):
        ref = pts.at[xx, zz, cc]
        return send(ref, ref, g_send.at[sem], g_recv.at[xx, zz, cc], device)

    for k in range(1, ZL):
        block(x, zl, core, (p, lax.rem(zl + k, ZL) * CORES + core), k).start()
    block(x, zl, core, sibling, 0).start()
    for j in range(1, X):
        block(x, zl, core, at_x(j), ZL - 1 + j).start()
    sem_zl = ZL + X - 1
    sem_x = sem_zl + (ZL - 1) * X

    square = (128, 128)
    eye = lax.broadcasted_iota(jnp.int32, square, 0) == lax.broadcasted_iota(jnp.int32, square, 1)
    loads[2].wait()

    def spread(g, carry):
        row = lax.rsqrt(counters[pl.ds(g, 1), :].astype(F32) + 1.0)
        col = jnp.sum(jnp.where(eye, row, 0.0), axis=1, keepdims=True)
        inv[pl.ds(pl.multiple_of(g * 128, 128), 128), :] = jnp.broadcast_to(col, square)
        return carry

    lax.fori_loop(0, counters.shape[0], spread, 0)
    loads[3].wait()

    def stat_copy(src, hh, k):
        ref = stats.at[src, hh]
        return send(ref, ref, s_send.at[k, hh], s_recv.at[src, hh], at_cells(k))

    def points_of(xx, hh):
        return pts[xx, pl.ds(hh * half_chips, half_chips)].reshape(lanes, width)

    def local_stats(hh):
        points = points_of(x, hh)

        def product(s, top):
            part = dot_nt(cent[s], points)
            tmp[s] = part
            return jnp.maximum(top, jnp.max(part, axis=0, keepdims=True))

        top = lax.fori_loop(0, X, product, jnp.full((1, lanes), -jnp.inf, F32))
        shift = top * scale

        def add_up(s, sums):
            expo = jnp.exp2(tmp[s] * scale - shift)
            weights = inv[pl.ds(pl.multiple_of(s * slice_rows, 128), slice_rows), :]
            weights = jnp.concatenate([weights] * (lanes // 128), axis=1)
            return (
                sums[0] + jnp.sum(expo, axis=0, keepdims=True),
                sums[1] + jnp.sum(expo * weights, axis=0, keepdims=True),
            )

        zero = jnp.zeros((1, lanes), F32)
        total, novel = lax.fori_loop(0, X, add_up, (zero, zero))
        stats[me, hh, 0:1, :] = top
        stats[me, hh, 1:2, :] = total
        stats[me, hh, 2:3, :] = novel

        def start(k, carry):
            stat_copy(me, hh, k).start()
            return carry

        lax.fori_loop(1, peers, start, 0)
        logit[x, :, pl.ds(pl.multiple_of(hh * lanes, 128), lanes)] = tmp[x]

    def forward(zz, slot):
        block(x, zz, core, sibling, 0).wait_recv()
        block(x, zz, core, sibling, sem_zl + slot * X).start()
        for j in range(1, X):
            block(x, zz, core, at_x(j), sem_zl + slot * X + j).start()

    begin = half * half_chips
    for k in range(1, half_chips):
        forward(begin + lax.rem(zl - begin + k, half_chips), k - 1)
    for k in range(half_chips):
        block(x, begin + k, other, sibling, 0).wait_recv()
    local_stats(half)
    begin = (1 - half) * half_chips
    for k in range(half_chips):
        forward(begin + k, half_chips - 1 + k)
    for k in range(half_chips):
        block(x, begin + k, other, sibling, 0).wait_recv()
    local_stats(1 - half)

    x_order = [1, 3, 2] if X == 4 else list(range(1, X))

    def pass_on(hh):
        for i, j in enumerate(x_order):
            xx = lax.rem(x + j, X)
            for k in range(half_chips):
                zz = hh * half_chips + k
                block(xx, zz, core, sibling, 0).wait_recv()
                block(xx, zz, core, sibling, sem_x + i * ZL + zz).start()

    def x_logits(j):
        xx = lax.rem(x + j, X)
        for zz in range(ZL):
            block(xx, zz, other, sibling, 0).wait_recv()
        logit[xx] = dot_nt(cent[x], pts[xx].reshape(line, width))

    pass_on(half)

    def stats_in(k, carry):
        src = lax.rem(me + k, peers)
        for hh in range(2):
            stat_copy(src, hh, k).wait_recv()
        return carry

    lax.fori_loop(1, peers, stats_in, 0)
    for hh in range(2):
        here = slice(hh * lanes, (hh + 1) * lanes)
        tops = stats[:, hh, 0, :]
        top = jnp.max(tops, axis=0, keepdims=True)
        ratio = jnp.exp2((tops - top) * scale)
        total = jnp.sum(stats[:, hh, 1, :] * ratio, axis=0, keepdims=True)
        novel = jnp.sum(stats[:, hh, 2, :] * ratio, axis=0, keepdims=True)
        rm[x, 0:1, here] = top * scale
        rm[x, 1:2, here] = novel / total / total

    def rm_copy(src, j):
        return send(rm.at[src], rm.at[src], r_send.at[j], r_recv.at[src], at_x(j))

    for j in range(1, X):
        rm_copy(x, j).start()

    acc[...] = jnp.zeros(acc.shape, F32)
    massacc[...] = jnp.zeros(massacc.shape, F32)

    def weigh(xx, slot):
        for q in range(line // 128):
            here = slice(q * 128, (q + 1) * 128)
            shift, factor = rm[xx, 0:1, here], rm[xx, 1:2, here]
            part = (jnp.exp2(logit[xx, :, here] * scale - shift) * factor).astype(BF16)
            share[slot][:, here] = part
            massacc[...] += part.astype(F32)

    def add_product(xx, slot):
        acc[...] += jnp.dot(
            share[slot][...], pts[xx].reshape(line, width), preferred_element_type=F32
        ).reshape(acc.shape)

    pass_on(1 - half)
    weigh(x, 0)
    add_product(x, 0)
    for j in x_order:
        x_logits(j)
    for j in x_order:
        rm_copy(lax.rem(x + j, X), j).wait_recv()
    for i, j in enumerate(x_order):
        weigh(lax.rem(x + j, X), i)
        if i > 0:
            add_product(lax.rem(x + x_order[i - 1], X), i - 1)
    add_product(lax.rem(x + x_order[-1], X), len(x_order) - 1)

    def y_copy(q, src, k, dst):
        return send(y_out[q].at[dst], y_in[q].at[src], y_send.at[q, k], y_recv.at[q, src], at_y(k))

    def z_copy(q, src, k, dst):
        return send(z_out[q].at[dst], z_in[q].at[src], z_send.at[q, k], z_recv.at[q, src], at_z(k))

    def yz_copy(q, src, k, dst):
        return send(
            yz_out[q].at[dst], yz_in[q].at[src], yz_send.at[q, k], yz_recv.at[q, src], at_z(k)
        )

    def zy_copy(q, src, k, dst):
        return send(
            zy_out[q].at[dst], zy_in[q].at[src], zy_send.at[q, k], zy_recv.at[q, src], at_y(k)
        )

    def my_copy(src, k):
        return send(m_out, my_in.at[src], my_send.at[k], my_recv.at[src], at_y(k))

    def mz_copy(src, k):
        return send(mz_out, mz_in.at[src], mz_send.at[k], mz_recv.at[src], at_z(k))

    def over_y(step, first=0):
        return lax.fori_loop(1, Y, step, first)

    def over_z(step, first=0):
        return lax.fori_loop(1, ZH, step, first)

    def y_first(q):
        def start(k, carry):
            dst = lax.rem(y + k, Y)
            y_out[q][dst] = acc[dst, :, *y_cuts[q]].astype(BF16)
            y_copy(q, y, k, dst).start()
            return carry

        over_y(start)

    def z_first(q):
        def start(k, carry):
            dst = lax.rem(zh + k, ZH)
            z_out[q][dst] = acc[:, dst, *z_cuts[q]].astype(BF16)
            z_copy(q, zh, k, dst).start()
            return carry

        over_z(start)

    def y_then_z(q):
        def add(k, total):
            src = lax.rem(y + k, Y)
            y_copy(q, src, k, src).wait_recv()
            return total + y_in[q][src].astype(F32)

        y_sum[q][...] = over_y(add, acc[y, :, *y_cuts[q]])

        def start(k, carry):
            dst = lax.rem(zh + k, ZH)
            yz_out[q][dst] = y_sum[q][dst].astype(BF16)
            yz_copy(q, zh, k, dst).start()
            return carry

        over_z(start)

    def z_then_y(q):
        def add(k, carry):
            src = lax.rem(zh + k, ZH)
            z_copy(q, src, k, src).wait_recv()
            z_sum[q][...] += z_in[q][src].astype(F32)
            return carry

        z_sum[q][...] = acc[:, zh, *z_cuts[q]]
        over_z(add)

        def start(k, carry):
            dst = lax.rem(y + k, Y)
            zy_out[q][dst] = z_sum[q][dst].astype(BF16)
            zy_copy(q, y, k, dst).start()
            return carry

        over_y(start)

    def finish_y(q):
        def add(k, total):
            src = lax.rem(zh + k, ZH)
            yz_copy(q, src, k, src).wait_recv()
            return total + yz_in[q][src].astype(F32)

        sums_ref[*y_cuts[q]] = over_z(add, y_sum[q][zh])

    def finish_z(q):
        def add(k, total):
            src = lax.rem(y + k, Y)
            zy_copy(q, src, k, src).wait_recv()
            return total + zy_in[q][src].astype(F32)

        sums_ref[*z_cuts[q]] = over_y(add, z_sum[q][y])

    for q in range(max(NY, NZ)):
        if q < NZ:
            z_first(q)
        if q < NY:
            y_first(q)

    m_out[...] = jnp.zeros(m_out.shape, F32)
    for g in range(slice_rows // 128):
        col = jnp.sum(massacc[g * 128 : (g + 1) * 128, :], axis=1, keepdims=True)
        m_out[g : g + 1, :] = jnp.sum(jnp.where(eye, col, 0.0), axis=0, keepdims=True)

    def my_start(k, carry):
        my_copy(y, k).start()
        return carry

    over_y(my_start)

    for q in range(max(NY, NZ)):
        if q == 0:
            for r in range(NZ):
                z_then_y(r)
        if q < NY:
            y_then_z(q)
        if q == 0:

            def my_add(k, total):
                src = lax.rem(y + k, Y)
                my_copy(src, k).wait_recv()
                return total + my_in[src]

            mass = over_y(my_add, m_out[...])
            mz_out[...] = mass

            def mz_start(k, carry):
                mz_copy(zh, k).start()
                return carry

            over_z(mz_start)

    def mz_add(k, total):
        src = lax.rem(zh + k, ZH)
        mz_copy(src, k).wait_recv()
        return total + mz_in[src]

    mass = over_z(mz_add, mass)
    per_row = 128 // z_rows
    place = y * ZH + zh
    at_line = lax.broadcasted_iota(jnp.int32, mass.shape, 0) == lax.div(place, per_row)
    picked = jnp.sum(jnp.where(at_line, mass, 0.0), axis=0, keepdims=True)
    which = lax.rem(place, per_row)
    answer = jnp.zeros((1, z_rows), F32)
    for q in range(per_row):
        answer = jnp.where(which == q, picked[:, q * z_rows : (q + 1) * z_rows], answer)
    mass_ref[...] = answer

    for q in range(max(NY, NZ)):
        if q < NY:
            finish_y(q)
        if q < NZ:
            finish_z(q)

    def sent_block(i, carry):
        block(x, zl, core, sibling, i).wait_send()
        return carry

    lax.fori_loop(0, g_send.shape[0], sent_block, 0)

    def sent_stats(k, carry):
        for hh in range(2):
            stat_copy(me, hh, k).wait_send()
        return carry

    lax.fori_loop(1, peers, sent_stats, 0)
    for j in range(1, X):
        rm_copy(x, j).wait_send()

    def sent_y(k, carry):
        dst = lax.rem(y + k, Y)
        for q in range(NY):
            y_copy(q, y, k, dst).wait_send()
        for q in range(NZ):
            zy_copy(q, y, k, dst).wait_send()
        my_copy(y, k).wait_send()
        return carry

    over_y(sent_y)

    def sent_z(k, carry):
        dst = lax.rem(zh + k, ZH)
        for q in range(NY):
            yz_copy(q, zh, k, dst).wait_send()
        for q in range(NZ):
            z_copy(q, zh, k, dst).wait_send()
        mz_copy(zh, k).wait_send()
        return carry

    over_z(sent_z)


def body(codes, exponents, centroids, counters):
    rows, width = codes.shape
    cells = centroids.shape[0]
    slice_rows = cells // X
    z_rows = slice_rows // Y // ZH
    line = ZL * CORES * rows
    lanes = line // 2
    peers = ZL * CORES

    def size(piece):
        (r0, r1), (c0, c1) = piece
        return (r1 - r0) * z_rows // HALVES, (c1 - c0) * width // QUARTERS

    y_sizes = [size(piece) for piece in Y_PIECES]
    z_sizes = [size(piece) for piece in Z_PIECES]
    scale = 4.0 / math.sqrt(width) * math.log2(math.e)
    vmem, dma = pltpu.VMEM, pltpu.SemaphoreType.DMA
    hbm = pl.BlockSpec(memory_space=pltpu.HBM)
    sums, mass = pl.pallas_call(
        functools.partial(kernel, scale),
        out_shape=(
            jax.ShapeDtypeStruct((z_rows, width), F32),
            jax.ShapeDtypeStruct((1, z_rows), F32),
        ),
        in_specs=[hbm] * 4,
        out_specs=(pl.BlockSpec(memory_space=vmem), pl.BlockSpec(memory_space=vmem)),
        scratch_shapes=[
            vmem((rows, width), jnp.int32),
            vmem((1, rows), jnp.int32),
            vmem((X, slice_rows, width), BF16),
            vmem((cells // 128, 128), jnp.int32),
            vmem((X, ZL, CORES, rows, width), BF16),
            vmem((cells, 128), F32),
            vmem((X, slice_rows, lanes), F32),
            vmem((X, slice_rows, line), F32),
            [vmem((slice_rows, line), BF16) for _ in range(X - 1)],
            vmem((Y, ZH, z_rows, width), F32),
            vmem((slice_rows, 128), F32),
            vmem((peers, 2, 4, lanes), F32),
            vmem((X, 2, line), F32),
            [vmem((Y, ZH, *size), BF16) for size in y_sizes],
            [vmem((Y, ZH, *size), BF16) for size in y_sizes],
            [vmem((ZH, *size), F32) for size in y_sizes],
            [vmem((ZH, *size), BF16) for size in y_sizes],
            [vmem((ZH, *size), BF16) for size in y_sizes],
            [vmem((ZH, Y, *size), BF16) for size in z_sizes],
            [vmem((ZH, Y, *size), BF16) for size in z_sizes],
            [vmem((Y, *size), F32) for size in z_sizes],
            [vmem((Y, *size), BF16) for size in z_sizes],
            [vmem((Y, *size), BF16) for size in z_sizes],
            vmem((8, 128), F32),
            vmem((Y, 8, 128), F32),
            vmem((8, 128), F32),
            vmem((ZH, 8, 128), F32),
            dma((4,)),
            dma((X + ZL - 1 + (ZL - 1) * X + (X - 1) * ZL,)),
            dma((X, ZL, CORES)),
            dma((peers, 2)),
            dma((peers, 2)),
            dma((X,)),
            dma((X,)),
            dma((NY, Y)),
            dma((NY, Y)),
            dma((NY, ZH)),
            dma((NY, ZH)),
            dma((NZ, ZH)),
            dma((NZ, ZH)),
            dma((NZ, Y)),
            dma((NZ, Y)),
            dma((Y,)),
            dma((Y,)),
            dma((ZH,)),
            dma((ZH,)),
        ],
        compiler_params=pltpu.CompilerParams(
            collective_id=0, has_side_effects=True, vmem_limit_bytes=48 << 20
        ),
    )(*(
        pltpu.with_memory_space_constraint(a, pltpu.HBM)
        for a in (
            codes,
            exponents.reshape(1, rows),
            centroids.reshape(X, slice_rows, width),
            counters.reshape(cells // 128, 128),
        )
    ))
    return sums[None], mass


def solution(mesh):
    in_specs = (P(("pts", "cells"), None), P(("pts", "cells")), P("cells", None), P("cells"))
    out_specs = (P("cells", "pts", None), P("cells", "pts"))
    return jax.shard_map(body, mesh=mesh, in_specs=in_specs, out_specs=out_specs, check_vma=False)
```
